256 devices in a mesh: dp: 16 (over x_lo, z), mp: 16 (over x_hi, y, core).
Axes of the slice: x: 4 (x_hi: 2, x_lo: 2; x = x_hi * 2 + x_lo), y: 4, z: 8, core: 2. Of those that a mesh axis runs over, the one named last changes fastest.
Arguments:
- stream_left: bfloat16 [2048, 6144], P(None, 'dp'), may hold values from -30 to 30
- stream_right: bfloat16 [2048, 6144], P(None, 'dp'), may hold values from -30 to 30
- scale_left: float32 [6144], P('dp'), may hold values from 0.1 to 1.9
- scale_right: float32 [6144], P('dp'), may hold values from 0.1 to 1.9
- expand_left: bfloat16 [6144, 12288], P('dp', 'mp'), may hold values from -0.078125 to 0.078125
- expand_right: bfloat16 [6144, 12288], P('dp', 'mp'), may hold values from -0.078125 to 0.078125
- shift_left: float32 [12288], P('mp'), may hold values from -3 to 3
- shift_right: float32 [12288], P('mp'), may hold values from -3 to 3
- project_left: bfloat16 [12288, 6144], P('mp', 'dp'), may hold values from -0.0546875 to 0.0546875
- project_right: bfloat16 [12288, 6144], P('mp', 'dp'), may hold values from -0.0546875 to 0.0546875
- offset_left: float32 [6144], P('dp'), may hold values from -3 to 3
- offset_right: float32 [6144], P('dp'), may hold values from -3 to 3
Outputs:
- after_left: bfloat16 [2048, 6144], P('mp', 'dp')
- after_right: bfloat16 [2048, 6144], P('mp', 'dp')
- correlation: float32 [6144, 6144], P('dp', 'mp')
The draws below stay inside these ranges and needn't reach their ends.
All inputs are finite; a program needn't handle non-finite values.
Results may differ from the reference program's by a relative error of at most 0.014.
Values may be sent and summed in bfloat16 or wider, within the bound.
A program may use at most 64 MiB of HBM per device.

```python
import math
import jax
import jax.numpy as jnp
from jax import lax

D = 6144
FF = 12288
TOKENS = 2048
N_DP = 16
N_MP = 16


def shared_parts(key):
    base = jax.random.fold_in(key, 101)
    common = jnp.clip(jax.random.normal(jax.random.fold_in(base, 1), (TOKENS, D)), -5.0, 5.0)
    column = jnp.exp(jax.random.uniform(jax.random.fold_in(base, 2), (D,), minval=math.log(0.3), maxval=math.log(3.0)))
    row_scale = jnp.exp(jax.random.uniform(jax.random.fold_in(base, 3), (TOKENS, 1), minval=math.log(0.5), maxval=math.log(2.0)))
    order = jax.random.permutation(jax.random.fold_in(base, 4), D)
    return (common, column, row_scale, order)


def own_noise(key, salt):
    return jnp.clip(jax.random.normal(jax.random.fold_in(key, salt), (TOKENS, D)), -5.0, 5.0)


def draw_stream_left(key, part):
    common, column, row_scale, order = shared_parts(key)
    noise = own_noise(key, 202)
    return (row_scale * (0.8 * common * column[None, :] + 0.6 * noise)).astype(jnp.bfloat16)


def draw_stream_right(key, part):
    common, column, row_scale, order = shared_parts(key)
    noise = own_noise(key, 303)
    moved = common[:, order] * column[order][None, :]
    return (row_scale * (0.8 * moved + 0.6 * noise)).astype(jnp.bfloat16)


def block_levels(stream_key, shape, cuts, least, top_value):
    level = 1.0
    for dim, shards_of in cuts:
        heights = jax.random.uniform(jax.random.fold_in(jax.random.fold_in(stream_key, 6), dim), (shards_of,), jnp.float32, least / len(cuts), top_value / len(cuts))
        level = level * jnp.repeat(jnp.exp(heights), shape[dim] // shards_of).reshape((-1,) + (1,) * (len(shape) - 1 - dim))
    return level


def gaussian(own_key, extent, width, limit, cuts=(), dtype=jnp.bfloat16):
    drawn = jax.random.normal(own_key, extent, jnp.float32) * width
    if len(cuts) > 0:
        drawn = block_levels(own_key, extent, cuts, -0.22, 0.18) * drawn
    return jnp.clip(drawn, min=-limit, max=limit).astype(dtype)


def setup_inputs(seed: int = 0) -> dict:
    splits = jax.random.split(jax.random.key(seed), 13)
    return {
        "stream_left": draw_stream_left(jax.random.fold_in(splits[12], 71), 0),
        "stream_right": draw_stream_right(jax.random.fold_in(splits[12], 71), 0),
        "scale_left": jnp.clip(1.0 + 0.18 * jax.random.normal(splits[2], (D,), jnp.float32), 0.1, 1.9),
        "scale_right": jnp.clip(1.0 + 0.18 * jax.random.normal(splits[3], (D,), jnp.float32), 0.1, 1.9),
        "expand_left": gaussian(splits[4], (D, FF), D ** -0.5, 0.078125, ((0, 16), (1, 16))),
        "expand_right": gaussian(splits[5], (D, FF), D ** -0.5, 0.078125, ((0, 16), (1, 16))),
        "shift_left": gaussian(splits[6], (FF,), 0.5, 3.0, ((0, 16),), jnp.float32),
        "shift_right": gaussian(splits[7], (FF,), 0.5, 3.0, ((0, 16),), jnp.float32),
        "project_left": gaussian(splits[8], (FF, D), FF ** -0.5, 0.0546875, ((0, 16), (1, 16))),
        "project_right": gaussian(splits[9], (FF, D), FF ** -0.5, 0.0546875, ((0, 16), (1, 16))),
        "offset_left": gaussian(splits[10], (D,), 0.5, 3.0, ((0, 16),), jnp.float32),
        "offset_right": gaussian(splits[11], (D,), 0.5, 3.0, ((0, 16),), jnp.float32),
    }


EPS = 1e-06

def blocked_product(left, right, blocks):
    rows = left.shape[0]
    inner = left.shape[1]
    size = inner // blocks
    lefts = left.reshape(rows, blocks, size).transpose(1, 0, 2)
    rights = right.reshape(blocks, size, right.shape[1])

    def step(total, pair):
        term = jnp.dot(pair[0], pair[1], preferred_element_type=jnp.float32)
        term = lax.optimization_barrier(term.astype(jnp.bfloat16))
        return (total + term.astype(jnp.float32), None)
    total, _ = lax.scan(step, jnp.zeros((rows, right.shape[1]), jnp.float32), (lefts, rights))
    return total

def branch(stream, scale, expand, shift, project, offset):
    values = stream.astype(jnp.float32)
    mean = lax.optimization_barrier(jnp.mean(values, axis=1, keepdims=True))
    var = lax.optimization_barrier(jnp.mean(values * values, axis=1, keepdims=True)) - mean * mean
    normed = ((values - mean) * lax.rsqrt(var + EPS) * scale).astype(jnp.bfloat16)
    pre = blocked_product(normed, expand, N_DP) + shift
    act = jax.nn.gelu(pre, approximate=False).astype(jnp.bfloat16)
    out = blocked_product(act, project, N_MP)
    return (values + offset + out).astype(jnp.bfloat16)

def reference(stream_left, stream_right, scale_left, scale_right, expand_left, expand_right, shift_left, shift_right, project_left, project_right, offset_left, offset_right):
    after_left = branch(stream_left, scale_left, expand_left, shift_left, project_left, offset_left)
    after_right = branch(stream_right, scale_right, expand_right, shift_right, project_right, offset_right)
    correlation = jnp.dot(after_left.T, after_right, preferred_element_type=jnp.float32) / TOKENS
    return (after_left, after_right, correlation)
```

```python
import functools

import jax
import jax.numpy as jnp
from jax import lax
from jax.experimental import pallas as pl
from jax.experimental.pallas import tpu as pltpu
from jax.sharding import PartitionSpec as P

EPS = 1e-06
F32 = jnp.float32
BF16 = jnp.bfloat16
MESH = pl.DeviceIdType.MESH

NZ, NY = 8, 4
TOK = 128
W = 384
HID = 768


class Slots:
    def __init__(self):
        self.count = 0

    def take(self, n):
        first = self.count
        self.count += n
        return first


SLOTS = Slots()
S_STAT1 = SLOTS.take(16)
S_STAT2 = SLOTS.take(16)
S_EXP = [SLOTS.take(1) for _ in range(2)]
S_PROJ = [SLOTS.take(1) for _ in range(2)]
S_GAIN = [SLOTS.take(1) for _ in range(2)]
S_STREAM = [SLOTS.take(2) for _ in range(2)]
S_RS = [SLOTS.take(14) for _ in range(2)]
S_AG = [SLOTS.take(8) for _ in range(2)]
S_CORE = [SLOTS.take(1) for _ in range(2)]
S_Y = [SLOTS.take(4) for _ in range(2)]
S_X = [SLOTS.take(3) for _ in range(2)]
S_LEFT = SLOTS.take(8)
S_LEFTC = SLOTS.take(8)
S_TURN = SLOTS.take(1)
S_PAIR = SLOTS.take(1)
S_RIGHT = SLOTS.take(8)
N_SEMS = SLOTS.count


def spread(row, size=TOK):
    return jnp.broadcast_to(row, (size, size)).T


def kernel(
    s_l, s_r, g_l, g_r, e_l, e_r, b_l, b_r, p_l, p_r, o_l, o_r,
    a_l, a_r, corr,
    st1, st2, r1, r2, xe, xp, xg, xs, nrm, rr, rsb, act, yb, cr, ys, yr, xt, xr, al, at,
    ssem, rsem,
):
    streams, gains, expands, shifts = (s_l, s_r), (g_l, g_r), (e_l, e_r), (b_l, b_r)
    projects, offsets, afters = (p_l, p_r), (o_l, o_r), (a_l, a_r)
    i, j = lax.axis_index("dp"), lax.axis_index("mp")
    xl, z = lax.div(i, 8), lax.rem(i, 8)
    xh, y, c = lax.div(j, 8), lax.rem(lax.div(j, 2), 4), lax.rem(j, 2)

    def dev(xl_, z_, xh_, y_, c_):
        return (xl_ * 8 + z_, xh_ * 8 + y_ * 2 + c_)

    def copy(src, dst, sem, to, rsem_at=None):
        return pltpu.make_async_remote_copy(
            src_ref=src,
            dst_ref=dst,
            send_sem=ssem.at[sem],
            recv_sem=rsem.at[sem if rsem_at is None else rsem_at],
            device_id=to,
            device_id_type=MESH,
        )

    x_peer = dev(1 - xl, z, xh, y, c)
    w_peer = dev(1 - xl, z, 1 - xh, y, c)
    c_peer = dev(xl, z, xh, y, 1 - c)
    z_next = dev(xl, lax.rem(z + 1, 8), xh, y, c)
    z_prev = dev(xl, lax.rem(z + 7, 8), xh, y, c)

    barrier = pltpu.get_barrier_semaphore()

    def greet(d, _):
        pl.semaphore_signal(barrier, inc=1, device_id=(lax.rem(i + d, 16), j), device_id_type=MESH)
        pl.semaphore_signal(barrier, inc=1, device_id=(i, lax.rem(j + d, 16)), device_id_type=MESH)
        return 0

    lax.fori_loop(1, 16, greet, 0)
    pl.semaphore_signal(barrier, inc=1, device_id=w_peer, device_id_type=MESH)

    @pl.when(i != j)
    def _():
        pl.semaphore_signal(barrier, inc=1, device_id=(j, i), device_id_type=MESH)
        pl.semaphore_wait(barrier, 32)

    @pl.when(i == j)
    def _():
        pl.semaphore_wait(barrier, 31)

    sent = []

    def start(cp):
        cp.start()
        sent.append(cp)
        return cp

    def stream_copy(k):
        rows = pl.multiple_of((1 - xl) * 1024 + c * 512, 512)
        return copy(
            streams[k].at[pl.ds(rows, 512)],
            xs.at[k, pl.ds(pl.multiple_of(c * 512, 512), 512)],
            S_STREAM[k],
            w_peer,
        )

    def stream_forward(k):
        part = xs.at[k, pl.ds(pl.multiple_of(c * 512, 512), 512)]
        return copy(part, part, S_STREAM[k] + 1, c_peer)

    str_cp = [stream_copy(k) for k in range(2)]
    exp_cp = [copy(expands[k], xe.at[k], S_EXP[k], x_peer) for k in range(2)]
    prj_cp = [copy(projects[k], xp.at[k], S_PROJ[k], x_peer) for k in range(2)]
    gain_cp = [copy(gains[k], xg.at[k], S_GAIN[k], x_peer) for k in range(2)]
    start(gain_cp[0])
    start(gain_cp[1])
    start(str_cp[0])
    start(exp_cp[0])

    mine = pl.ds(pl.multiple_of(j * TOK, TOK), TOK)
    st1[...] = jnp.zeros((8, TOK), F32)
    for k in range(2):
        v = streams[k][mine, :].astype(F32)
        for n, col in enumerate((v, v * v)):
            total = jnp.sum(col, axis=1, keepdims=True)
            st1[2 * k + n : 2 * k + n + 1, :] = jnp.broadcast_to(total, (TOK, TOK)).T[0:1, :]
    r1[0] = st1[...]

    def stat1(d):
        return copy(st1, r1.at[d], S_STAT1 + d, (lax.rem(i + d, 16), j))

    def stat2(d):
        return copy(st2, r2.at[j], S_STAT2 + d, (i, lax.rem(j + d, 16)))

    def run(fn, lo=1, hi=16):
        def body(d, _):
            fn(d)
            return 0

        lax.fori_loop(lo, hi, body, 0)

    run(lambda d: stat1(d).start())
    run(lambda d: stat1(d).wait_recv())
    totals = r1[0]
    for d in range(1, 16):
        totals = totals + r1[d]
    totals = totals * (1.0 / 6144.0)
    st2[...] = jnp.zeros((8, TOK), F32)
    for k in range(2):
        mean = totals[2 * k : 2 * k + 1, :]
        var = totals[2 * k + 1 : 2 * k + 2, :] - mean * mean
        st2[2 * k : 2 * k + 1, :] = mean
        st2[2 * k + 1 : 2 * k + 2, :] = lax.rsqrt(var + EPS)
    r2[j] = st2[...]
    run(lambda d: stat2(d).start())
    run(lambda d: stat2(d).wait_recv())

    def normalise(k, part, r):
        t = xl * 8 + r
        stats = r2[t]
        mean = spread(stats[2 * k : 2 * k + 1, :])
        rstd = spread(stats[2 * k + 1 : 2 * k + 2, :])
        if part == 0:
            v = streams[k][pl.ds(pl.multiple_of(t * TOK, TOK), TOK), :]
            gain = gains[k][...]
        else:
            v = xs[k, pl.ds(pl.multiple_of(r * TOK, TOK), TOK), :]
            gain = xg[k]
        mean, rstd = (jnp.concatenate([q, q, q], axis=1) for q in (mean, rstd))
        nrm[k, r, part] = ((v.astype(F32) - mean) * rstd * gain).astype(BF16)

    def stream_in(k):
        str_cp[k].wait_recv()
        start(stream_forward(k))

    gain_cp[0].wait_recv()
    gain_cp[1].wait_recv()
    run(lambda r: normalise(0, 0, r), 0, 8)
    stream_in(0)
    start(str_cp[1])
    stream_forward(0).wait_recv()
    run(lambda r: normalise(0, 1, r), 0, 8)
    exp_cp[0].wait_recv()
    start(exp_cp[1])

    def cols(h):
        return slice(h * W, (h + 1) * W)

    def partial_pre(k, r, h):
        own = jnp.dot(nrm[k, r, 0], expands[k][:, cols(h)], preferred_element_type=F32)
        return own + jnp.dot(nrm[k, r, 1], xe[k, :, cols(h)], preferred_element_type=F32)

    def rs_copy(k, s, h):
        return copy(rsb.at[k, s, h], rr.at[k, s, h], S_RS[k] + 2 * s + h, (z_next, z_prev)[h])

    def rs_step(k, s, first=False):
        for h in range(2):
            r = lax.rem(z + 7 - s + 8, 8) if h == 0 else lax.rem(z + 1 + s, 8)
            acc = partial_pre(k, r, h)
            if not first:
                rs_copy(k, s - 1, h).wait_recv()
                acc = acc + rr[k, s - 1, h].astype(F32)
            rsb[k, s, h] = acc.astype(BF16)
            rs_copy(k, s, h).start()

    def rs_finish(k):
        for h in range(2):
            acc = partial_pre(k, z, h) + shifts[k][:, cols(h)]
            rs_copy(k, 6, h).wait_recv()
            acc = acc + rr[k, 6, h].astype(F32)
            act[k, z, h] = (0.5 * acc * (1.0 + lax.erf(acc * (0.5 ** 0.5)))).astype(BF16)

    def ag_copy(k, s, way):
        if way == 0:
            r, to = lax.rem(z - s + 8, 8), z_next
        else:
            r, to = lax.rem(z + s, 8), z_prev
        ref = act.at[k, r, way] if isinstance(s, int) and s == 3 else act.at[k, r]
        return copy(ref, ref, S_AG[k] + 2 * s + way, to)

    def ag_step(k, s, first=False):
        for way in range(2):
            if not first:
                ag_copy(k, s - 1, way).wait_recv()
            ag_copy(k, s, way).start()

    def ag_finish(k):
        for way in range(2):
            ag_copy(k, 3, way).wait_recv()

    def gemm2(k, r):
        for b, weight in enumerate((projects[k], xp.at[k])):
            out = jnp.dot(act[k, r, 0], weight[0:W, :], preferred_element_type=F32)
            out = out + jnp.dot(act[k, r, 1], weight[W:HID, :], preferred_element_type=F32)
            yb[k, lax.rem(r, 2), lax.div(r, 2), b] = out.astype(BF16)

    def core_copy(k):
        return copy(yb.at[k, 1 - c], cr.at[k], S_CORE[k], c_peer)

    def y_copy(k, d):
        return copy(ys.at[k, d - 1], yr.at[k, d - 1], S_Y[k] + d, dev(xl, z, xh, lax.rem(y + d, 4), c))

    def chip_sum(k, t):
        return yb[k, c, t].astype(F32) + cr[k, t].astype(F32)

    def y_start(k):
        core_copy(k).wait_recv()
        for d in (2, 1, 3):
            ys[k, d - 1] = chip_sum(k, lax.rem(y + d, 4)).astype(BF16)
            start(y_copy(k, d))

    def x_copy_a(k):
        return copy(
            xt.at[k, 1], xr.at[k, xh], S_X[k], dev(1 - xl, z, xl, y, c), S_X[k] + xh
        )

    def x_copy_a_in(k, n):
        return copy(xt.at[k, 1], xr.at[k, n], S_X[k], x_peer, S_X[k] + n)

    def x_copy_b(k):
        return copy(xt.at[k, 0], xr.at[k, 2], S_X[k] + 2, dev(xl, z, 1 - xh, y, c))

    def x_start(k):
        total = chip_sum(k, y)
        for d in (1, 3, 2):
            y_copy(k, d).wait_recv()
            total = total + yr[k, d - 1].astype(F32)
        xt[k] = total.astype(BF16)
        start(x_copy_a(k))

        @pl.when(xh != xl)
        def _():
            x_copy_b(k).start()

    def finish(k):
        def put(branch):
            resid = streams[k][mine, :].astype(F32) + offsets[k][...]
            afters[k][...] = (resid + branch).astype(BF16)

        @pl.when(xh != xl)
        def _():
            x_copy_a_in(k, 0).wait_recv()
            x_copy_a_in(k, 1).wait_recv()
            put(xr[k, 0].astype(F32) + xr[k, 1].astype(F32))
            x_copy_b(k).wait_send()

        @pl.when(xh == xl)
        def _():
            x_copy_b(k).wait_recv()
            put(xt[k, 0].astype(F32) + xr[k, 2].astype(F32))

    rs_step(0, 0, True)
    run(lambda s: rs_step(0, s), 1, 7)
    stream_in(1)
    exp_cp[1].wait_recv()
    start(prj_cp[0])
    start(prj_cp[1])
    run(lambda r: normalise(1, 0, r), 0, 8)
    stream_forward(1).wait_recv()
    run(lambda r: normalise(1, 1, r), 0, 8)
    rs_finish(0)

    ag_step(0, 0, True)
    rs_step(1, 0, True)

    def both(q, _):
        rs_step(1, 2 * q + 1)
        ag_step(0, q + 1)
        rs_step(1, 2 * q + 2)
        return 0

    lax.fori_loop(0, 2, both, 0)
    ag_step(0, 3)
    run(lambda s: rs_step(1, s), 5, 7)
    rs_finish(1)

    ag_step(1, 0, True)
    ag_finish(0)
    prj_cp[0].wait_recv()
    run(lambda r: gemm2(0, r), 0, 8)
    start(core_copy(0))
    ag_step(1, 1)
    y_start(0)
    ag_step(1, 2)
    x_start(0)
    ag_step(1, 3)
    finish(0)

    q = xh * 4 + y
    al[j] = a_l[...]

    def left_copy(d):
        to = lax.rem(q + d, 8)
        return copy(a_l, al.at[j], S_LEFT + d, (i, to * 2 + c))

    def left_forward(d):
        ref = al.at[lax.rem(q - d + 8, 8) * 2 + c]
        return copy(ref, ref, S_LEFTC + d, c_peer)

    run(lambda d: left_copy(d).start(), 1, 8)
    left_forward(0).start()
    ag_finish(1)
    prj_cp[1].wait_recv()
    run(lambda r: gemm2(1, r), 0, 8)
    start(core_copy(1))
    y_start(1)

    def left_pass(d):
        left_copy(d).wait_recv()
        left_forward(d).start()

    run(left_pass, 1, 8)
    x_start(1)
    finish(1)

    here = at.at[z, xl]
    turn = copy(a_r, at.at[lax.rem(j, 8), lax.div(j, 8)], S_TURN, (j, i))

    @pl.when(i != j)
    def _():
        turn.start()
        turn.wait()

    @pl.when(i == j)
    def _():
        at[z, xl] = a_r[...]

    pair = start(copy(here, here, S_PAIR, x_peer))
    pair.wait_recv()

    def right_copy(s, way):
        if way == 0:
            r, to = lax.rem(z - s + 8, 8), z_next
        else:
            r, to = lax.rem(z + s, 8), z_prev
        ref = at.at[r, way] if s == 3 else at.at[r]
        return copy(ref, ref, S_RIGHT + 2 * s + way, to)

    def add(r, first=False):
        total = None
        for n in range(2):
            term = lax.dot_general(
                al[n * 8 + r], at[r, n], (((0,), (0,)), ((), ())), preferred_element_type=F32
            )
            total = term if total is None else total + term
        corr[...] = total if first else corr[...] + total

    for way in range(2):
        start(right_copy(0, way))
    run(lambda d: left_forward(d).wait_recv(), 0, 8)
    add(z, True)
    for s in range(1, 4):
        for way in range(2):
            right_copy(s - 1, way).wait_recv()
            start(right_copy(s, way))
        add(lax.rem(z - s + 8, 8))
        add(lax.rem(z + s, 8))
    for way in range(2):
        right_copy(3, way).wait_recv()
    add(lax.rem(z + 4, 8))
    corr[...] = corr[...] * (1.0 / 2048.0)

    for cp in sent:
        cp.wait_send()
    run(lambda d: stat1(d).wait_send())
    run(lambda d: stat2(d).wait_send())
    for k in range(2):
        for h in range(2):
            run(lambda s: rs_copy(k, s, h).wait_send(), 0, 7)
            for s in range(4):
                ag_copy(k, s, h).wait_send()
    run(lambda d: left_copy(d).wait_send(), 1, 8)
    run(lambda d: left_forward(d).wait_send(), 0, 8)


def per_device(s_l, s_r, g_l, g_r, e_l, e_r, b_l, b_r, p_l, p_r, o_l, o_r):
    row = lambda v: v.reshape(1, -1)
    vm = pl.BlockSpec(memory_space=pltpu.VMEM)
    tile = (TOK, W)
    return pl.pallas_call(
        kernel,
        out_shape=(
            jax.ShapeDtypeStruct(tile, BF16),
            jax.ShapeDtypeStruct(tile, BF16),
            jax.ShapeDtypeStruct((W, W), F32),
        ),
        in_specs=[vm] * 12,
        out_specs=(vm, vm, vm),
        scratch_shapes=[
            pltpu.VMEM((8, TOK), F32),
            pltpu.VMEM((8, TOK), F32),
            pltpu.VMEM((16, 8, TOK), F32),
            pltpu.VMEM((16, 8, TOK), F32),
            pltpu.VMEM((2, W, HID), BF16),
            pltpu.VMEM((2, HID, W), BF16),
            pltpu.VMEM((2, 1, W), F32),
            pltpu.VMEM((2, 1024, W), BF16),
            pltpu.VMEM((2, 8, 2) + tile, BF16),
            pltpu.VMEM((2, 7, 2) + tile, BF16),
            pltpu.VMEM((2, 7, 2) + tile, BF16),
            pltpu.VMEM((2, 8, 2) + tile, BF16),
            pltpu.VMEM((2, 2, 4, 2) + tile, BF16),
            pltpu.VMEM((2, 4, 2) + tile, BF16),
            pltpu.VMEM((2, 3, 2) + tile, BF16),
            pltpu.VMEM((2, 3, 2) + tile, BF16),
            pltpu.VMEM((2, 2) + tile, BF16),
            pltpu.VMEM((2, 3) + tile, BF16),
            pltpu.VMEM((16,) + tile, BF16),
            pltpu.VMEM((8, 2) + tile, BF16),
            pltpu.SemaphoreType.DMA((N_SEMS,)),
            pltpu.SemaphoreType.DMA((N_SEMS,)),
        ],
        compiler_params=pltpu.CompilerParams(
            collective_id=0, has_side_effects=True, vmem_limit_bytes=56 * 1024 * 1024
        ),
    )(s_l, s_r, row(g_l), row(g_r), e_l, e_r, row(b_l), row(b_r), p_l, p_r, row(o_l), row(o_r))


def solution(mesh):
    placed = (
        P(None, "dp"),
        P(None, "dp"),
        P("dp"),
        P("dp"),
        P("dp", "mp"),
        P("dp", "mp"),
        P("mp"),
        P("mp"),
        P("mp", "dp"),
        P("mp", "dp"),
        P("dp"),
        P("dp"),
    )
    return jax.shard_map(
        per_device,
        mesh=mesh,
        in_specs=placed,
        out_specs=(P("mp", "dp"), P("mp", "dp"), P("dp", "mp")),
        check_vma=False,
    )
```

```python
import functools

import jax
import jax.numpy as jnp
from jax import lax
from jax.experimental import pallas as pl
from jax.experimental.pallas import tpu as pltpu
from jax.sharding import PartitionSpec as P

EPS = 1e-06
F32 = jnp.float32
BF16 = jnp.bfloat16
MESH = pl.DeviceIdType.MESH

NZ, NY = 8, 4
TOK = 128
W = 384
HID = 768


class Slots:
    def __init__(self):
        self.count = 0

    def take(self, n):
        first = self.count
        self.count += n
        return first


SLOTS = Slots()
S_STAT1 = SLOTS.take(16)
S_STAT2 = SLOTS.take(16)
S_EXP = [SLOTS.take(1) for _ in range(2)]
S_PROJ = [SLOTS.take(1) for _ in range(2)]
S_GAIN = [SLOTS.take(1) for _ in range(2)]
S_STREAM = [SLOTS.take(2) for _ in range(2)]
S_RS = [SLOTS.take(28) for _ in range(2)]
S_AG = [SLOTS.take(16) for _ in range(2)]
S_CORE = [SLOTS.take(1) for _ in range(2)]
S_Y = [SLOTS.take(4) for _ in range(2)]
S_X = [SLOTS.take(3) for _ in range(2)]
S_LEFT = SLOTS.take(8)
S_LEFTC = SLOTS.take(8)
S_TURN = SLOTS.take(1)
S_PAIR = SLOTS.take(1)
S_RIGHT = SLOTS.take(16)
N_SEMS = SLOTS.count


def spread(row, size=TOK):
    return jnp.broadcast_to(row, (size, size)).T


def kernel(
    s_l, s_r, g_l, g_r, e_l, e_r, b_l, b_r, p_l, p_r, o_l, o_r,
    a_l, a_r, corr,
    st1, st2, r1, r2, xe, xp, xg0, xg1, xs, nrm, rr, rsb, act, yb, cr, ys, yr, xt, xr, al, at,
    sc, sv, ev, pv, ssem, rsem, lsem,
):
    streams, gains, expands, shifts = (s_l, s_r), (g_l, g_r), (e_l, e_r), (b_l, b_r)
    projects, offsets, afters, xg = (p_l, p_r), (o_l, o_r), (a_l, a_r), (xg0, xg1)
    i, j = lax.axis_index("dp"), lax.axis_index("mp")
    xl, z = lax.div(i, 8), lax.rem(i, 8)
    xh, y, c = lax.div(j, 8), lax.rem(lax.div(j, 2), 4), lax.rem(j, 2)

    def dev(xl_, z_, xh_, y_, c_):
        return (xl_ * 8 + z_, xh_ * 8 + y_ * 2 + c_)

    def copy(src, dst, sem, to, rsem_at=None):
        return pltpu.make_async_remote_copy(
            src_ref=src,
            dst_ref=dst,
            send_sem=ssem.at[sem],
            recv_sem=rsem.at[sem if rsem_at is None else rsem_at],
            device_id=to,
            device_id_type=MESH,
        )

    x_peer = dev(1 - xl, z, xh, y, c)
    w_peer = dev(1 - xl, z, 1 - xh, y, c)
    c_peer = dev(xl, z, xh, y, 1 - c)
    z_next = dev(xl, lax.rem(z + 1, 8), xh, y, c)
    z_prev = dev(xl, lax.rem(z + 7, 8), xh, y, c)

    share = y * 2 + c

    def token_rows(h):
        return pl.ds(pl.multiple_of((h * 8 + share) * TOK, TOK), TOK)

    stat_in = [
        pltpu.make_async_copy(streams[k].at[token_rows(h)], sc.at[k, h], lsem.at[k * 2 + h])
        for k in range(2)
        for h in range(2)
    ]
    stream_in_own = [pltpu.make_async_copy(streams[k], sv.at[k], lsem.at[4 + k]) for k in range(2)]
    expand_in = [pltpu.make_async_copy(expands[k], ev.at[k], lsem.at[6 + k]) for k in range(2)]
    project_in = [pltpu.make_async_copy(projects[k], pv.at[k], lsem.at[8 + k]) for k in range(2)]
    for cp in stat_in + stream_in_own[:1] + expand_in + stream_in_own[1:] + project_in:
        cp.start()

    barrier = pltpu.get_barrier_semaphore()

    def greet(d, _):
        pl.semaphore_signal(barrier, inc=1, device_id=(lax.rem(i + d, 16), j), device_id_type=MESH)
        pl.semaphore_signal(barrier, inc=1, device_id=(i, lax.rem(j + d, 16)), device_id_type=MESH)
        return 0

    lax.fori_loop(1, 16, greet, 0)
    pl.semaphore_signal(barrier, inc=1, device_id=w_peer, device_id_type=MESH)

    @pl.when(i != j)
    def _():
        pl.semaphore_signal(barrier, inc=1, device_id=(j, i), device_id_type=MESH)

    for k in range(2):
        for h in range(2):
            stat_in[k * 2 + h].wait()
            v = sc[k, h].astype(F32)
            for n, col in enumerate((v, v * v)):
                total = jnp.sum(col, axis=1, keepdims=True)
                at_row = h * 4 + k * 2 + n
                st1[at_row : at_row + 1, :] = jnp.broadcast_to(total, (TOK, TOK)).T[0:1, :]
    r1[0] = st1[...]

    @pl.when(i != j)
    def _():
        pl.semaphore_wait(barrier, 32)

    @pl.when(i == j)
    def _():
        pl.semaphore_wait(barrier, 31)

    sent, ends = [], []

    def drain():
        for cp in sent:
            cp.wait_send()
        for end in ends:
            end()

    def start(cp):
        cp.start()
        sent.append(cp)
        return cp

    def stream_copy(k):
        rows = pl.multiple_of((1 - xl) * 1024 + c * 512, 512)
        return copy(
            streams[k].at[pl.ds(rows, 512)],
            xs.at[k, pl.ds(pl.multiple_of(c * 512, 512), 512)],
            S_STREAM[k],
            w_peer,
        )

    def stream_forward(k):
        part = xs.at[k, pl.ds(pl.multiple_of(c * 512, 512), 512)]
        return copy(part, part, S_STREAM[k] + 1, c_peer)

    str_cp = [stream_copy(k) for k in range(2)]
    exp_cp = [copy(expands[k], xe.at[k], S_EXP[k], x_peer) for k in range(2)]
    prj_cp = [copy(projects[k], xp.at[k], S_PROJ[k], x_peer) for k in range(2)]
    gain_cp = [copy(gains[k], xg[k], S_GAIN[k], x_peer) for k in range(2)]
    mine = pl.ds(pl.multiple_of(j * TOK, TOK), TOK)

    def stat1(d):
        return copy(st1, r1.at[d], S_STAT1 + d, (lax.rem(i + d, 16), j))

    def stat2(d):
        return copy(st2, r2.at[share], S_STAT2 + d, (i, xh * 8 + lax.rem(share + d, 8)))

    def run(fn, lo=1, hi=16):
        def body(d, _):
            fn(d)
            return 0

        lax.fori_loop(lo, hi, body, 0)

    run(lambda d: stat1(d).start())
    ends.append(lambda: run(lambda d: stat1(d).wait_send()))
    start(gain_cp[0])
    start(gain_cp[1])
    start(str_cp[0])
    start(exp_cp[0])
    run(lambda d: stat1(d).wait_recv())
    totals = r1[0]
    for d in range(1, 16):
        totals = totals + r1[d]
    totals = totals * (1.0 / 6144.0)
    totals = jnp.where(xl == 0, totals[0:4, :], totals[4:8, :])
    st2[...] = jnp.zeros((8, TOK), F32)
    for k in range(2):
        mean = totals[2 * k : 2 * k + 1, :]
        var = totals[2 * k + 1 : 2 * k + 2, :] - mean * mean
        st2[2 * k : 2 * k + 1, :] = mean
        st2[2 * k + 1 : 2 * k + 2, :] = lax.rsqrt(var + EPS)
    r2[share] = st2[...]
    run(lambda d: stat2(d).start(), 1, 8)
    ends.append(lambda: run(lambda d: stat2(d).wait_send(), 1, 8))
    run(lambda d: stat2(d).wait_recv(), 1, 8)

    def normalise(k, part, r):
        t = xl * 8 + r
        stats = r2[r]
        mean = spread(stats[2 * k : 2 * k + 1, :])
        rstd = spread(stats[2 * k + 1 : 2 * k + 2, :])
        if part == 0:
            v = sv[k, pl.ds(pl.multiple_of(t * TOK, TOK), TOK), :]
            gain = gains[k][...]
        else:
            v = xs[k, pl.ds(pl.multiple_of(r * TOK, TOK), TOK), :]
            gain = xg[k][...]
        mean, rstd = (jnp.concatenate([q, q, q], axis=1) for q in (mean, rstd))
        nrm[k, r, part] = ((v.astype(F32) - mean) * rstd * gain.reshape(1, W)).astype(BF16)

    def stream_in(k):
        str_cp[k].wait_recv()
        start(stream_forward(k))

    gain_cp[0].wait_recv()
    gain_cp[1].wait_recv()
    stream_in_own[0].wait()
    run(lambda r: normalise(0, 0, r), 0, 8)
    stream_in(0)
    start(str_cp[1])
    stream_forward(0).wait_recv()
    run(lambda r: normalise(0, 1, r), 0, 8)
    exp_cp[0].wait_recv()
    start(exp_cp[1])
    expand_in[0].wait()
    stream_in_own[1].wait()

    def cols(h):
        return slice(h * W, (h + 1) * W)

    def partial_pre(k, r, h):
        own = jnp.dot(nrm[k, r, 0], ev[k, :, cols(h)], preferred_element_type=F32)
        return own + jnp.dot(nrm[k, r, 1], xe[k, :, cols(h)], preferred_element_type=F32)

    def part(ref, u):
        return ref.at[pl.ds(u * 64, 64)]

    def rs_copy(k, s, h, u):
        sem = S_RS[k] + 4 * s + 2 * h + u
        return copy(part(rsb.at[k, s, h], u), part(rr.at[k, s, h], u), sem, (z_next, z_prev)[h])

    def rs_step(k, s, first=False):
        own = [
            partial_pre(k, lax.rem(z + 7 - s + 8, 8) if h == 0 else lax.rem(z + 1 + s, 8), h)
            for h in range(2)
        ]
        for u in range(2):
            rows = slice(u * 64, (u + 1) * 64)
            for h in range(2):
                acc = own[h][rows]
                if not first:
                    rs_copy(k, s - 1, h, u).wait_recv()
                    acc = acc + rr[k, s - 1, h, rows].astype(F32)
                rsb[k, s, h, rows] = acc.astype(BF16)
                rs_copy(k, s, h, u).start()

    def rs_sent(k):
        for h in range(2):
            for u in range(2):
                run(lambda s: rs_copy(k, s, h, u).wait_send(), 0, 7)

    def rs_finish(k):
        for h in range(2):
            acc = partial_pre(k, z, h) + shifts[k][cols(h)].reshape(1, W)
            for u in range(2):
                rs_copy(k, 6, h, u).wait_recv()
            acc = acc + rr[k, 6, h].astype(F32)
            act[k, z, h] = (0.5 * acc * (1.0 + lax.erf(acc * (0.5 ** 0.5)))).astype(BF16)

    def ag_copy(k, s, way, half):
        if way == 0:
            r, to = lax.rem(z - s + 8, 8), z_next
        else:
            r, to = lax.rem(z + s, 8), z_prev
        ref = act.at[k, r, half]
        return copy(ref, ref, S_AG[k] + 4 * s + 2 * way + half, to)

    def ag_step(k, s, first=False, last=False):
        for half in range(2):
            for way in range(2):
                if not first:
                    ag_copy(k, s - 1, way, half).wait_recv()
                if not last or half == way:
                    ag_copy(k, s, way, half).start()

    def ag_finish(k):
        for way in range(2):
            ag_copy(k, 3, way, way).wait_recv()

    def ag_sent(k):
        for way in range(2):
            for half in range(2):
                run(lambda s: ag_copy(k, s, way, half).wait_send(), 0, 3)
            ag_copy(k, 3, way, way).wait_send()

    def gemm2(k, r):
        for b, weight in enumerate((pv.at[k], xp.at[k])):
            out = jnp.dot(act[k, r, 0], weight[0:W, :], preferred_element_type=F32)
            out = out + jnp.dot(act[k, r, 1], weight[W:HID, :], preferred_element_type=F32)
            yb[k, lax.rem(r, 2), lax.div(r, 2), b] = out.astype(BF16)

    def core_copy(k):
        return copy(yb.at[k, 1 - c], cr.at[k], S_CORE[k], c_peer)

    def y_copy(k, d):
        return copy(ys.at[k, d - 1], yr.at[k, d - 1], S_Y[k] + d, dev(xl, z, xh, lax.rem(y + d, 4), c))

    def chip_sum(k, t):
        return yb[k, c, t].astype(F32) + cr[k, t].astype(F32)

    def y_start(k):
        core_copy(k).wait_recv()
        for d in (2, 1, 3):
            ys[k, d - 1] = chip_sum(k, lax.rem(y + d, 4)).astype(BF16)
            start(y_copy(k, d))

    def x_copy_a(k):
        return copy(
            xt.at[k, 1], xr.at[k, xh], S_X[k], dev(1 - xl, z, xl, y, c), S_X[k] + xh
        )

    def x_copy_a_in(k, n):
        return copy(xt.at[k, 1], xr.at[k, n], S_X[k], x_peer, S_X[k] + n)

    def x_copy_b(k):
        return copy(xt.at[k, 0], xr.at[k, 2], S_X[k] + 2, dev(xl, z, 1 - xh, y, c))

    def x_start(k):
        total = chip_sum(k, y)
        for d in (1, 3, 2):
            y_copy(k, d).wait_recv()
            total = total + yr[k, d - 1].astype(F32)
        xt[k] = total.astype(BF16)
        start(x_copy_a(k))

        @pl.when(xh != xl)
        def _():
            x_copy_b(k).start()

    def finish(k):
        def put(branch):
            resid = sv[k, mine, :].astype(F32) + offsets[k][...].reshape(1, W)
            afters[k][...] = (resid + branch).astype(BF16)

        @pl.when(xh != xl)
        def _():
            x_copy_a_in(k, 0).wait_recv()
            x_copy_a_in(k, 1).wait_recv()
            put(xr[k, 0].astype(F32) + xr[k, 1].astype(F32))
            x_copy_b(k).wait_send()

        @pl.when(xh == xl)
        def _():
            x_copy_b(k).wait_recv()
            put(xt[k, 0].astype(F32) + xr[k, 2].astype(F32))

    rs_step(0, 0, True)

    def own_part(s):
        rs_step(0, s)
        normalise(1, 0, 2 * s - 2)
        normalise(1, 0, 2 * s - 1)

    run(own_part, 1, 5)
    stream_in(1)
    exp_cp[1].wait_recv()
    start(prj_cp[0])
    start(prj_cp[1])
    expand_in[1].wait()
    stream_forward(1).wait_recv()

    def peer_part(s):
        rs_step(0, s)
        run(lambda n: normalise(1, 1, 4 * (s - 5) + n), 0, 4)

    run(peer_part, 5, 7)
    ends.append(lambda: rs_sent(0))

    rs_step(1, 0, True)
    rs_finish(0)
    ag_step(0, 0, True)

    def both(q, _):
        rs_step(1, 2 * q + 1)
        ag_step(0, q + 1)
        rs_step(1, 2 * q + 2)
        return 0

    lax.fori_loop(0, 2, both, 0)
    rs_step(1, 5)
    ag_step(0, 3, last=True)
    rs_step(1, 6)
    ends.append(lambda: rs_sent(1))
    ends.append(lambda: ag_sent(0))
    rs_finish(1)

    def gemm2_pair(k, s):
        gemm2(k, lax.rem(z - s + 8, 8))
        gemm2(k, lax.rem(z + s, 8))

    ag_step(1, 0, True)
    ag_finish(0)
    project_in[0].wait()
    project_in[1].wait()
    prj_cp[0].wait_recv()
    run(lambda r: gemm2(0, r), 0, 8)
    start(core_copy(0))
    ag_step(1, 1)
    y_start(0)
    prj_cp[1].wait_recv()
    gemm2(1, z)
    gemm2_pair(1, 1)
    ag_step(1, 2)
    gemm2_pair(1, 2)
    ag_step(1, 3, last=True)
    x_start(0)
    gemm2_pair(1, 3)
    ag_finish(1)
    ends.append(lambda: ag_sent(1))
    gemm2(1, lax.rem(z + 4, 8))
    start(core_copy(1))
    finish(0)

    place = xh * 4 + y
    y_start(1)
    al[share, xh] = a_l[...]

    def left_copy(d):
        to = lax.rem(place + d, 8)
        return copy(a_l, al.at[share, xh], S_LEFT + d, (i, to * 2 + c))

    def left_forward(d):
        came = lax.rem(place - d + 8, 8)
        ref = al.at[lax.rem(came, 4) * 2 + c, lax.div(came, 4)]
        return copy(ref, ref, S_LEFTC + d, c_peer)

    run(lambda d: left_copy(d).start(), 1, 8)
    left_forward(0).start()
    ends.append(lambda: run(lambda d: left_copy(d).wait_send(), 1, 8))
    ends.append(lambda: run(lambda d: left_forward(d).wait_send(), 0, 8))
    x_start(1)
    finish(1)

    turn = copy(a_r, at.at[lax.rem(j, 8), lax.div(j, 8)], S_TURN, (j, i))

    @pl.when(i != j)
    def _():
        turn.start()

    @pl.when(i == j)
    def _():
        at[z, xl] = a_r[...]

    def left_pass(d):
        left_copy(d).wait_recv()
        left_forward(d).start()

    run(left_pass, 1, 8)

    @pl.when(i != j)
    def _():
        turn.wait()

    here = at.at[z, xl]
    pair = start(copy(here, here, S_PAIR, x_peer))

    def right_copy(s, way, which):
        if way == 0:
            r, to = lax.rem(z - s + 8, 8), z_next
        else:
            r, to = lax.rem(z + s, 8), z_prev
        ref = at.at[r, xl if which == 0 else 1 - xl]
        return copy(ref, ref, S_RIGHT + 4 * s + 2 * way + which, to)

    def add(r, first=False):
        term = lax.dot_general(
            al[r].reshape(2 * TOK, W),
            at[r].reshape(2 * TOK, W),
            (((0,), (0,)), ((), ())),
            preferred_element_type=F32,
        )
        corr[...] = term if first else corr[...] + term

    for way in range(2):
        start(right_copy(0, way, 0))
    pair.wait_recv()
    for way in range(2):
        start(right_copy(0, way, 1))
    run(lambda d: left_forward(d).wait_recv(), 0, 8)
    add(z, True)
    for s in range(1, 4):
        for which in range(2):
            for way in range(2):
                right_copy(s - 1, way, which).wait_recv()
                if s < 3 or way == which:
                    start(right_copy(s, way, which))
        add(lax.rem(z - s + 8, 8))
        add(lax.rem(z + s, 8))
    for way in range(2):
        right_copy(3, way, way).wait_recv()
    add(lax.rem(z + 4, 8))
    corr[...] = corr[...] * (1.0 / 2048.0)
    drain()


def hand_out(a_l, a_r, corr, a_l_out, a_r_out, corr_out, sems):
    copies = [
        pltpu.make_async_copy(src, dst, sems.at[n])
        for n, (src, dst) in enumerate(((corr, corr_out), (a_l, a_l_out), (a_r, a_r_out)))
    ]
    for cp in copies:
        cp.start()
    for cp in copies:
        cp.wait()


def per_device(s_l, s_r, g_l, g_r, e_l, e_r, b_l, b_r, p_l, p_r, o_l, o_r):
    vm = pl.BlockSpec(memory_space=pltpu.VMEM)
    hbm = pl.BlockSpec(memory_space=pl.ANY)
    tile = (TOK, W)
    shapes = (
        jax.ShapeDtypeStruct(tile, BF16),
        jax.ShapeDtypeStruct(tile, BF16),
        jax.ShapeDtypeStruct((W, W), F32),
    )
    results = pl.pallas_call(
        kernel,
        out_shape=shapes,
        in_specs=[hbm, hbm, vm, vm, hbm, hbm, vm, vm, hbm, hbm, vm, vm],
        out_specs=(vm, vm, vm),
        scratch_shapes=[
            pltpu.VMEM((8, TOK), F32),
            pltpu.VMEM((8, TOK), F32),
            pltpu.VMEM((16, 8, TOK), F32),
            pltpu.VMEM((8, 8, TOK), F32),
            pltpu.VMEM((2, W, HID), BF16),
            pltpu.VMEM((2, HID, W), BF16),
            pltpu.VMEM((W,), F32),
            pltpu.VMEM((W,), F32),
            pltpu.VMEM((2, 1024, W), BF16),
            pltpu.VMEM((2, 8, 2) + tile, BF16),
            pltpu.VMEM((2, 7, 2) + tile, BF16),
            pltpu.VMEM((2, 7, 2) + tile, BF16),
            pltpu.VMEM((2, 8, 2) + tile, BF16),
            pltpu.VMEM((2, 2, 4, 2) + tile, BF16),
            pltpu.VMEM((2, 4, 2) + tile, BF16),
            pltpu.VMEM((2, 3, 2) + tile, BF16),
            pltpu.VMEM((2, 3, 2) + tile, BF16),
            pltpu.VMEM((2, 2) + tile, BF16),
            pltpu.VMEM((2, 3) + tile, BF16),
            pltpu.VMEM((8, 2) + tile, BF16),
            pltpu.VMEM((8, 2) + tile, BF16),
            pltpu.VMEM((2, 2) + tile, BF16),
            pltpu.VMEM((2, 2048, W), BF16),
            pltpu.VMEM((2, W, HID), BF16),
            pltpu.VMEM((2, HID, W), BF16),
            pltpu.SemaphoreType.DMA((N_SEMS,)),
            pltpu.SemaphoreType.DMA((N_SEMS,)),
            pltpu.SemaphoreType.DMA((10,)),
        ],
        compiler_params=pltpu.CompilerParams(
            collective_id=0, has_side_effects=True, vmem_limit_bytes=56 * 1024 * 1024
        ),
    )(s_l, s_r, g_l, g_r, e_l, e_r, b_l, b_r, p_l, p_r, o_l, o_r)
    return pl.pallas_call(
        hand_out,
        out_shape=shapes,
        in_specs=[hbm] * 3,
        out_specs=(hbm,) * 3,
        scratch_shapes=[pltpu.SemaphoreType.DMA((3,))],
    )(*results)


def solution(mesh):
    placed = (
        P(None, "dp"),
        P(None, "dp"),
        P("dp"),
        P("dp"),
        P("dp", "mp"),
        P("dp", "mp"),
        P("mp"),
        P("mp"),
        P("mp", "dp"),
        P("mp", "dp"),
        P("dp"),
        P("dp"),
    )
    return jax.shard_map(
        per_device,
        mesh=mesh,
        in_specs=placed,
        out_specs=(P("mp", "dp"), P("mp", "dp"), P("dp", "mp")),
        check_vma=False,
    )
```

```python
import functools

import jax
import jax.numpy as jnp
from jax import lax
from jax.experimental import pallas as pl
from jax.experimental.pallas import tpu as pltpu
from jax.sharding import PartitionSpec as P

EPS = 1e-06
F32 = jnp.float32
BF16 = jnp.bfloat16
MESH = pl.DeviceIdType.MESH

NZ, NY = 8, 4
TOK = 128
W = 384
HID = 768


class Slots:
    def __init__(self):
        self.count = 0

    def take(self, n):
        first = self.count
        self.count += n
        return first


SLOTS = Slots()
S_STAT1 = SLOTS.take(16)
S_STAT2 = SLOTS.take(16)
S_EXP = [SLOTS.take(2) for _ in range(2)]
S_PROJ = [SLOTS.take(1) for _ in range(2)]
S_GAIN = [SLOTS.take(1) for _ in range(2)]
S_STREAM = [SLOTS.take(16) for _ in range(2)]
S_RS = [SLOTS.take(16) for _ in range(2)]
S_AG = [SLOTS.take(16) for _ in range(2)]
S_CORE = [SLOTS.take(1) for _ in range(2)]
S_Y = [SLOTS.take(4) for _ in range(2)]
S_X = [SLOTS.take(3) for _ in range(2)]
S_LEFT = SLOTS.take(8)
S_LEFTC = SLOTS.take(8)
S_TURN = SLOTS.take(1)
S_PAIR = SLOTS.take(1)
S_RIGHT = SLOTS.take(16)
N_SEMS = SLOTS.count


def spread(row, size=TOK):
    return jnp.broadcast_to(row, (size, size)).T


def kernel(
    s_l, s_r, g_l, g_r, e_l, e_r, b_l, b_r, p_l, p_r, o_l, o_r,
    a_l, a_r, corr,
    st1, st2, r1, r2, xe, xp, xg0, xg1, xs, nrm, rr, rsb, act, yb, cr, ys, yr, xt, xr, al, at,
    sc, sv, ev, pv, ssem, rsem, lsem,
):
    streams, gains, expands, shifts = (s_l, s_r), (g_l, g_r), (e_l, e_r), (b_l, b_r)
    projects, offsets, afters, xg = (p_l, p_r), (o_l, o_r), (a_l, a_r), (xg0, xg1)
    i, j = lax.axis_index("dp"), lax.axis_index("mp")
    xl, z = lax.div(i, 8), lax.rem(i, 8)
    xh, y, c = lax.div(j, 8), lax.rem(lax.div(j, 2), 4), lax.rem(j, 2)

    def dev(xl_, z_, xh_, y_, c_):
        return (xl_ * 8 + z_, xh_ * 8 + y_ * 2 + c_)

    def copy(src, dst, sem, to, rsem_at=None):
        return pltpu.make_async_remote_copy(
            src_ref=src,
            dst_ref=dst,
            send_sem=ssem.at[sem],
            recv_sem=rsem.at[sem if rsem_at is None else rsem_at],
            device_id=to,
            device_id_type=MESH,
        )

    x_peer = dev(1 - xl, z, xh, y, c)
    w_peer = dev(1 - xl, z, 1 - xh, y, c)
    c_peer = dev(xl, z, xh, y, 1 - c)
    z_next = dev(xl, lax.rem(z + 1, 8), xh, y, c)
    z_prev = dev(xl, lax.rem(z + 7, 8), xh, y, c)

    share = y * 2 + c

    def token_rows(h):
        return pl.ds(pl.multiple_of((h * 8 + share) * TOK, TOK), TOK)

    stat_in = [
        pltpu.make_async_copy(streams[k].at[token_rows(h)], sc.at[k, h], lsem.at[k * 2 + h])
        for k in range(2)
        for h in range(2)
    ]
    stream_in_own = [pltpu.make_async_copy(streams[k], sv.at[k], lsem.at[4 + k]) for k in range(2)]
    expand_in = [pltpu.make_async_copy(expands[k], ev.at[k], lsem.at[6 + k]) for k in range(2)]
    project_in = [pltpu.make_async_copy(projects[k], pv.at[k], lsem.at[8 + k]) for k in range(2)]
    for cp in stat_in + stream_in_own[:1] + expand_in + stream_in_own[1:] + project_in:
        cp.start()

    barrier = pltpu.get_barrier_semaphore()

    def greet(d, _):
        pl.semaphore_signal(barrier, inc=1, device_id=(lax.rem(i + d, 16), j), device_id_type=MESH)
        pl.semaphore_signal(barrier, inc=1, device_id=(i, lax.rem(j + d, 16)), device_id_type=MESH)
        return 0

    lax.fori_loop(1, 16, greet, 0)
    pl.semaphore_signal(barrier, inc=1, device_id=w_peer, device_id_type=MESH)

    @pl.when(i != j)
    def _():
        pl.semaphore_signal(barrier, inc=1, device_id=(j, i), device_id_type=MESH)

    for k in range(2):
        for h in range(2):
            stat_in[k * 2 + h].wait()
            v = sc[k, h].astype(F32)
            for n, col in enumerate((v, v * v)):
                total = jnp.sum(col, axis=1, keepdims=True)
                at_row = h * 4 + k * 2 + n
                st1[at_row : at_row + 1, :] = jnp.broadcast_to(total, (TOK, TOK)).T[0:1, :]
    r1[0] = st1[...]

    @pl.when(i != j)
    def _():
        pl.semaphore_wait(barrier, 32)

    @pl.when(i == j)
    def _():
        pl.semaphore_wait(barrier, 31)

    sent, ends = [], []

    def drain():
        for cp in sent:
            cp.wait_send()
        for end in ends:
            end()

    def start(cp):
        cp.start()
        sent.append(cp)
        return cp

    def nth_chunk(n):
        return lax.rem(z + 4 + (1 - 2 * lax.rem(n, 2)) * lax.div(n + 1, 2) + 8, 8)

    half_rows = pl.ds(pl.multiple_of(c * 64, 64), 64)

    def stream_copy(k, n):
        r = nth_chunk(n)
        rows = pl.multiple_of(((1 - xl) * 8 + r) * TOK + c * 64, 64)
        return copy(
            streams[k].at[pl.ds(rows, 64)], xs.at[k, r, half_rows], S_STREAM[k] + n, w_peer
        )

    def stream_forward(k, n):
        piece = xs.at[k, nth_chunk(n), half_rows]
        return copy(piece, piece, S_STREAM[k] + 8 + n, c_peer)

    def cols(h):
        return slice(h * W, (h + 1) * W)

    exp_cp = [
        [copy(expands[k].at[:, cols(h)], xe.at[k, h], S_EXP[k] + h, x_peer) for h in range(2)]
        for k in range(2)
    ]
    prj_cp = [copy(projects[k], xp.at[k], S_PROJ[k], x_peer) for k in range(2)]
    gain_cp = [copy(gains[k], xg[k], S_GAIN[k], x_peer) for k in range(2)]
    mine = pl.ds(pl.multiple_of(j * TOK, TOK), TOK)

    def stat1(d):
        return copy(st1, r1.at[d], S_STAT1 + d, (lax.rem(i + d, 16), j))

    def stat2(d):
        return copy(st2, r2.at[share], S_STAT2 + d, (i, xh * 8 + lax.rem(share + d, 8)))

    def run(fn, lo=1, hi=16):
        def body(d, _):
            fn(d)
            return 0

        lax.fori_loop(lo, hi, body, 0)

    run(lambda d: stat1(d).start())
    ends.append(lambda: run(lambda d: stat1(d).wait_send()))
    start(gain_cp[0])
    start(gain_cp[1])
    start(exp_cp[0][0])
    run(lambda n: stream_copy(0, n).start(), 0, 8)
    start(exp_cp[0][1])
    run(lambda d: stat1(d).wait_recv())
    totals = r1[0]
    for d in range(1, 16):
        totals = totals + r1[d]
    totals = totals * (1.0 / 6144.0)
    totals = jnp.where(xl == 0, totals[0:4, :], totals[4:8, :])
    st2[...] = jnp.zeros((8, TOK), F32)
    for k in range(2):
        mean = totals[2 * k : 2 * k + 1, :]
        var = totals[2 * k + 1 : 2 * k + 2, :] - mean * mean
        st2[2 * k : 2 * k + 1, :] = mean
        st2[2 * k + 1 : 2 * k + 2, :] = lax.rsqrt(var + EPS)
    r2[share] = st2[...]
    run(lambda d: stat2(d).start(), 1, 8)
    ends.append(lambda: run(lambda d: stat2(d).wait_send(), 1, 8))
    run(lambda d: stat2(d).wait_recv(), 1, 8)

    def normalise(k, part, r):
        t = xl * 8 + r
        stats = r2[r]
        mean = spread(stats[2 * k : 2 * k + 1, :])
        rstd = spread(stats[2 * k + 1 : 2 * k + 2, :])
        if part == 0:
            v = sv[k, pl.ds(pl.multiple_of(t * TOK, TOK), TOK), :]
            gain = gains[k][...]
        else:
            v = xs[k, r]
            gain = xg[k][...]
        mean, rstd = (jnp.concatenate([q, q, q], axis=1) for q in (mean, rstd))
        nrm[k, r, part] = ((v.astype(F32) - mean) * rstd * gain.reshape(1, W)).astype(BF16)

    def pass_on(k, lo, hi):
        def one(n):
            stream_copy(k, n).wait_recv()
            stream_forward(k, n).start()

        run(one, lo, hi)

    def prepare(k, lo, hi):
        def one(n):
            stream_forward(k, n).wait_recv()
            normalise(k, 1, nth_chunk(n))

        run(one, lo, hi)

    def partial_pre(k, r, h):
        own = jnp.dot(nrm[k, r, 0], ev[k, :, cols(h)], preferred_element_type=F32)
        return own + jnp.dot(nrm[k, r, 1], xe[k, h], preferred_element_type=F32)

    def rs_copy(k, s, way, half):
        sem = S_RS[k] + 4 * s + 2 * way + half
        return copy(rsb.at[k, s, way, half], rr.at[k, s, way, half], sem, (z_next, z_prev)[way])

    def rs_step(k, s, half):
        for way in range(2):
            if s == 0 and half != way:
                continue
            r = lax.rem(z + 4 - s + 8, 8) if way == 0 else lax.rem(z + 4 + s, 8)
            acc = partial_pre(k, r, half)
            if s > 1 or (s == 1 and half == way):
                rs_copy(k, s - 1, way, half).wait_recv()
                acc = acc + rr[k, s - 1, way, half].astype(F32)
            rsb[k, s, way, half] = acc.astype(BF16)
            rs_copy(k, s, way, half).start()

    def rs_sent(k):
        for way in range(2):
            rs_copy(k, 0, way, way).wait_send()
            for half in range(2):
                run(lambda s: rs_copy(k, s, way, half).wait_send(), 1, 4)

    def rs_finish(k):
        for half in range(2):
            acc = partial_pre(k, z, half) + shifts[k][cols(half)].reshape(1, W)
            for way in range(2):
                rs_copy(k, 3, way, half).wait_recv()
                acc = acc + rr[k, 3, way, half].astype(F32)
            act[k, z, half] = (0.5 * acc * (1.0 + lax.erf(acc * (0.5 ** 0.5)))).astype(BF16)

    def ag_copy(k, s, way, half):
        if way == 0:
            r, to = lax.rem(z - s + 8, 8), z_next
        else:
            r, to = lax.rem(z + s, 8), z_prev
        ref = act.at[k, r, half]
        return copy(ref, ref, S_AG[k] + 4 * s + 2 * way + half, to)

    def ag_step(k, s, first=False, last=False):
        for half in range(2):
            for way in range(2):
                if not first:
                    ag_copy(k, s - 1, way, half).wait_recv()
                if not last or half == way:
                    ag_copy(k, s, way, half).start()

    def ag_finish(k):
        for way in range(2):
            ag_copy(k, 3, way, way).wait_recv()

    def ag_sent(k):
        for way in range(2):
            for half in range(2):
                run(lambda s: ag_copy(k, s, way, half).wait_send(), 0, 3)
            ag_copy(k, 3, way, way).wait_send()

    def gemm2(k, r):
        for b, weight in enumerate((pv.at[k], xp.at[k])):
            out = jnp.dot(act[k, r, 0], weight[0:W, :], preferred_element_type=F32)
            out = out + jnp.dot(act[k, r, 1], weight[W:HID, :], preferred_element_type=F32)
            yb[k, lax.rem(r, 2), lax.div(r, 2), b] = out.astype(BF16)

    def core_copy(k):
        return copy(yb.at[k, 1 - c], cr.at[k], S_CORE[k], c_peer)

    def y_copy(k, d):
        return copy(ys.at[k, d - 1], yr.at[k, d - 1], S_Y[k] + d, dev(xl, z, xh, lax.rem(y + d, 4), c))

    def chip_sum(k, t):
        return yb[k, c, t].astype(F32) + cr[k, t].astype(F32)

    def y_start(k):
        core_copy(k).wait_recv()
        for d in (2, 1, 3):
            ys[k, d - 1] = chip_sum(k, lax.rem(y + d, 4)).astype(BF16)
            start(y_copy(k, d))

    def x_copy_a(k):
        return copy(
            xt.at[k, 1], xr.at[k, xh], S_X[k], dev(1 - xl, z, xl, y, c), S_X[k] + xh
        )

    def x_copy_a_in(k, n):
        return copy(xt.at[k, 1], xr.at[k, n], S_X[k], x_peer, S_X[k] + n)

    def x_copy_b(k):
        return copy(xt.at[k, 0], xr.at[k, 2], S_X[k] + 2, dev(xl, z, 1 - xh, y, c))

    def x_start(k):
        total = chip_sum(k, y)
        for d in (1, 3, 2):
            y_copy(k, d).wait_recv()
            total = total + yr[k, d - 1].astype(F32)
        xt[k] = total.astype(BF16)
        start(x_copy_a(k))

        @pl.when(xh != xl)
        def _():
            x_copy_b(k).start()

    def finish(k):
        def put(branch):
            resid = sv[k, mine, :].astype(F32) + offsets[k][...].reshape(1, W)
            afters[k][...] = (resid + branch).astype(BF16)

        @pl.when(xh != xl)
        def _():
            x_copy_a_in(k, 0).wait_recv()
            x_copy_a_in(k, 1).wait_recv()
            put(xr[k, 0].astype(F32) + xr[k, 1].astype(F32))
            x_copy_b(k).wait_send()

        @pl.when(xh == xl)
        def _():
            x_copy_b(k).wait_recv()
            put(xt[k, 0].astype(F32) + xr[k, 2].astype(F32))

    gain_cp[0].wait_recv()
    gain_cp[1].wait_recv()
    stream_in_own[0].wait()
    expand_in[0].wait()
    pass_on(0, 0, 3)
    run(lambda r: normalise(0, 0, r), 0, 8)
    prepare(0, 0, 3)
    exp_cp[0][0].wait_recv()
    rs_step(0, 0, 0)
    pass_on(0, 3, 8)
    run(lambda n: stream_copy(1, n).start(), 0, 8)
    rs_step(0, 1, 0)
    prepare(0, 3, 5)
    exp_cp[0][1].wait_recv()
    start(exp_cp[1][0])
    start(exp_cp[1][1])
    rs_step(0, 0, 1)
    rs_step(0, 2, 0)
    prepare(0, 5, 8)
    rs_step(0, 1, 1)
    rs_step(0, 3, 0)
    stream_in_own[1].wait()
    run(lambda r: normalise(1, 0, r), 0, 8)
    rs_step(0, 2, 1)
    pass_on(1, 0, 8)
    rs_step(0, 3, 1)
    prepare(1, 0, 8)
    for k in range(2):
        ends.append(lambda k=k: run(lambda n: stream_copy(k, n).wait_send(), 0, 8))
        ends.append(lambda k=k: run(lambda n: stream_forward(k, n).wait_send(), 0, 8))
    ends.append(lambda: rs_sent(0))

    rs_finish(0)
    ag_step(0, 0, True)
    expand_in[1].wait()
    exp_cp[1][0].wait_recv()
    rs_step(1, 0, 0)
    exp_cp[1][1].wait_recv()
    start(prj_cp[0])
    rs_step(1, 0, 1)
    for s in range(1, 4):
        ag_step(0, s, last=s == 3)
        rs_step(1, s, 0)
        rs_step(1, s, 1)
        if s == 2:
            start(prj_cp[1])
    ends.append(lambda: rs_sent(1))
    ends.append(lambda: ag_sent(0))
    rs_finish(1)

    def gemm2_pair(k, s):
        gemm2(k, lax.rem(z - s + 8, 8))
        gemm2(k, lax.rem(z + s, 8))

    ag_step(1, 0, True)
    ag_finish(0)
    project_in[0].wait()
    project_in[1].wait()
    prj_cp[0].wait_recv()
    run(lambda r: gemm2(0, r), 0, 8)
    start(core_copy(0))
    ag_step(1, 1)
    y_start(0)
    prj_cp[1].wait_recv()
    gemm2(1, z)
    gemm2_pair(1, 1)
    ag_step(1, 2)
    gemm2_pair(1, 2)
    ag_step(1, 3, last=True)
    x_start(0)
    gemm2_pair(1, 3)
    ag_finish(1)
    ends.append(lambda: ag_sent(1))
    gemm2(1, lax.rem(z + 4, 8))
    start(core_copy(1))
    finish(0)

    place = xh * 4 + y
    y_start(1)
    al[share, xh] = a_l[...]

    def left_copy(d):
        to = lax.rem(place + d, 8)
        return copy(a_l, al.at[share, xh], S_LEFT + d, (i, to * 2 + c))

    def left_forward(d):
        came = lax.rem(place - d + 8, 8)
        ref = al.at[lax.rem(came, 4) * 2 + c, lax.div(came, 4)]
        return copy(ref, ref, S_LEFTC + d, c_peer)

    x_start(1)
    finish(1)

    turn = copy(a_r, at.at[lax.rem(j, 8), lax.div(j, 8)], S_TURN, (j, i))

    @pl.when(i != j)
    def _():
        turn.start()

    @pl.when(i == j)
    def _():
        at[z, xl] = a_r[...]

    run(lambda d: left_copy(d).start(), 1, 8)
    left_forward(0).start()
    ends.append(lambda: run(lambda d: left_copy(d).wait_send(), 1, 8))
    ends.append(lambda: run(lambda d: left_forward(d).wait_send(), 0, 8))

    def left_pass(d):
        left_copy(d).wait_recv()
        left_forward(d).start()

    @pl.when(i != j)
    def _():
        turn.wait()

    here = at.at[z, xl]
    pair = start(copy(here, here, S_PAIR, x_peer))

    def right_copy(s, way, which):
        if way == 0:
            r, to = lax.rem(z - s + 8, 8), z_next
        else:
            r, to = lax.rem(z + s, 8), z_prev
        ref = at.at[r, xl if which == 0 else 1 - xl]
        return copy(ref, ref, S_RIGHT + 4 * s + 2 * way + which, to)

    def add(r, first=False):
        term = lax.dot_general(
            al[r].reshape(2 * TOK, W),
            at[r].reshape(2 * TOK, W),
            (((0,), (0,)), ((), ())),
            preferred_element_type=F32,
        )
        corr[...] = term if first else corr[...] + term

    def pass_right(s):
        for which in range(2):
            for way in range(2):
                right_copy(s - 1, way, which).wait_recv()
                if s < 3 or way == which:
                    start(right_copy(s, way, which))

    def add_pair(s):
        add(lax.rem(z - s + 8, 8))
        add(lax.rem(z + s, 8))

    for way in range(2):
        start(right_copy(0, way, 0))
    pair.wait_recv()
    for way in range(2):
        start(right_copy(0, way, 1))
    run(left_pass, 1, 4)
    pass_right(1)
    run(left_pass, 4, 8)
    pass_right(2)
    run(lambda d: left_forward(d).wait_recv(), 0, 8)
    add(z, True)
    add_pair(1)
    pass_right(3)
    add_pair(2)
    add_pair(3)
    for way in range(2):
        right_copy(3, way, way).wait_recv()
    add(lax.rem(z + 4, 8))
    drain()


def hand_out(a_l, a_r, corr, a_l_out, a_r_out, corr_out):
    a_l_out[...] = a_l[...]
    a_r_out[...] = a_r[...]
    corr_out[...] = corr[...] * (1.0 / 2048.0)


def per_device(s_l, s_r, g_l, g_r, e_l, e_r, b_l, b_r, p_l, p_r, o_l, o_r):
    vm = pl.BlockSpec(memory_space=pltpu.VMEM)
    hbm = pl.BlockSpec(memory_space=pl.ANY)
    tile = (TOK, W)
    shapes = (
        jax.ShapeDtypeStruct(tile, BF16),
        jax.ShapeDtypeStruct(tile, BF16),
        jax.ShapeDtypeStruct((W, W), F32),
    )
    results = pl.pallas_call(
        kernel,
        out_shape=shapes,
        in_specs=[hbm, hbm, vm, vm, hbm, hbm, vm, vm, hbm, hbm, vm, vm],
        out_specs=(vm, vm, vm),
        scratch_shapes=[
            pltpu.VMEM((8, TOK), F32),
            pltpu.VMEM((8, TOK), F32),
            pltpu.VMEM((16, 8, TOK), F32),
            pltpu.VMEM((8, 8, TOK), F32),
            pltpu.VMEM((2, 2, W, W), BF16),
            pltpu.VMEM((2, HID, W), BF16),
            pltpu.VMEM((W,), F32),
            pltpu.VMEM((W,), F32),
            pltpu.VMEM((2, 8) + tile, BF16),
            pltpu.VMEM((2, 8, 2) + tile, BF16),
            pltpu.VMEM((2, 4, 2, 2) + tile, BF16),
            pltpu.VMEM((2, 4, 2, 2) + tile, BF16),
            pltpu.VMEM((2, 8, 2) + tile, BF16),
            pltpu.VMEM((2, 2, 4, 2) + tile, BF16),
            pltpu.VMEM((2, 4, 2) + tile, BF16),
            pltpu.VMEM((2, 3, 2) + tile, BF16),
            pltpu.VMEM((2, 3, 2) + tile, BF16),
            pltpu.VMEM((2, 2) + tile, BF16),
            pltpu.VMEM((2, 3) + tile, BF16),
            pltpu.VMEM((8, 2) + tile, BF16),
            pltpu.VMEM((8, 2) + tile, BF16),
            pltpu.VMEM((2, 2) + tile, BF16),
            pltpu.VMEM((2, 2048, W), BF16),
            pltpu.VMEM((2, W, HID), BF16),
            pltpu.VMEM((2, HID, W), BF16),
            pltpu.SemaphoreType.DMA((N_SEMS,)),
            pltpu.SemaphoreType.DMA((N_SEMS,)),
            pltpu.SemaphoreType.DMA((10,)),
        ],
        compiler_params=pltpu.CompilerParams(
            collective_id=0, has_side_effects=True, vmem_limit_bytes=56 * 1024 * 1024
        ),
    )(s_l, s_r, g_l, g_r, e_l, e_r, b_l, b_r, p_l, p_r, o_l, o_r)
    return pl.pallas_call(
        hand_out,
        out_shape=shapes,
        in_specs=[vm] * 3,
        out_specs=(vm,) * 3,
    )(*results)


def solution(mesh):
    placed = (
        P(None, "dp"),
        P(None, "dp"),
        P("dp"),
        P("dp"),
        P("dp", "mp"),
        P("dp", "mp"),
        P("mp"),
        P("mp"),
        P("mp", "dp"),
        P("mp", "dp"),
        P("dp"),
        P("dp"),
    )
    return jax.shard_map(
        per_device,
        mesh=mesh,
        in_specs=placed,
        out_specs=(P("mp", "dp"), P("mp", "dp"), P("dp", "mp")),
        check_vma=False,
    )
```

```python
import functools

import jax
import jax.numpy as jnp
from jax import lax
from jax.experimental import pallas as pl
from jax.experimental.pallas import tpu as pltpu
from jax.sharding import PartitionSpec as P

EPS = 1e-06
F32 = jnp.float32
BF16 = jnp.bfloat16
MESH = pl.DeviceIdType.MESH

NZ, NY = 8, 4
TOK = 128
W = 384
HID = 768


class Slots:
    def __init__(self):
        self.count = 0

    def take(self, n):
        first = self.count
        self.count += n
        return first


SLOTS = Slots()
S_STAT1 = SLOTS.take(16)
S_STAT2 = SLOTS.take(16)
S_EXP = [SLOTS.take(2) for _ in range(2)]
S_PROJ = [SLOTS.take(1) for _ in range(2)]
S_GAIN = [SLOTS.take(1) for _ in range(2)]
S_STREAM = [SLOTS.take(16) for _ in range(2)]
S_RS = [SLOTS.take(16) for _ in range(2)]
S_AG = [SLOTS.take(16) for _ in range(2)]
S_CORE = [SLOTS.take(2) for _ in range(2)]
S_Y = [SLOTS.take(8) for _ in range(2)]
S_X = [SLOTS.take(3) for _ in range(2)]
S_LEFT = SLOTS.take(8)
S_LEFTC = SLOTS.take(8)
S_TURN = SLOTS.take(1)
S_PAIR = SLOTS.take(1)
S_RIGHT = SLOTS.take(16)
S_CROSS = SLOTS.take(3)
N_SEMS = SLOTS.count


def spread(row, size=TOK):
    return jnp.broadcast_to(row, (size, size)).T


def kernel(
    s_l, s_r, g_l, g_r, e_l, e_r, b_l, b_r, p_l, p_r, o_l, o_r,
    a_l, a_r, corr,
    st1, st2, r1, r2, xe, xp, xg0, xg1, xs, nrm, rr, rsb, act, yb, cr, ys, yr, xt, xr, al, at,
    sc, sv, ev, pv, ssem, rsem, lsem,
):
    streams, gains, expands, shifts = (s_l, s_r), (g_l, g_r), (e_l, e_r), (b_l, b_r)
    projects, offsets, afters, xg = (p_l, p_r), (o_l, o_r), (a_l, a_r), (xg0, xg1)
    i, j = lax.axis_index("dp"), lax.axis_index("mp")
    xl, z = lax.div(i, 8), lax.rem(i, 8)
    xh, y, c = lax.div(j, 8), lax.rem(lax.div(j, 2), 4), lax.rem(j, 2)

    def dev(xl_, z_, xh_, y_, c_):
        return (xl_ * 8 + z_, xh_ * 8 + y_ * 2 + c_)

    def copy(src, dst, sem, to, rsem_at=None):
        return pltpu.make_async_remote_copy(
            src_ref=src,
            dst_ref=dst,
            send_sem=ssem.at[sem],
            recv_sem=rsem.at[sem if rsem_at is None else rsem_at],
            device_id=to,
            device_id_type=MESH,
        )

    x_peer = dev(1 - xl, z, xh, y, c)
    w_peer = dev(1 - xl, z, 1 - xh, y, c)
    c_peer = dev(xl, z, xh, y, 1 - c)
    z_next = dev(xl, lax.rem(z + 1, 8), xh, y, c)
    z_prev = dev(xl, lax.rem(z + 7, 8), xh, y, c)

    share = y * 2 + c

    def token_rows(h):
        return pl.ds(pl.multiple_of((h * 8 + share) * TOK, TOK), TOK)

    stat_in = [
        pltpu.make_async_copy(streams[k].at[token_rows(h)], sc.at[k, h], lsem.at[k * 2 + h])
        for k in range(2)
        for h in range(2)
    ]
    stream_in_own = [pltpu.make_async_copy(streams[k], sv.at[k], lsem.at[4 + k]) for k in range(2)]
    expand_in = [pltpu.make_async_copy(expands[k], ev.at[k], lsem.at[6 + k]) for k in range(2)]
    project_in = [pltpu.make_async_copy(projects[k], pv.at[k], lsem.at[8 + k]) for k in range(2)]
    for cp in stat_in + stream_in_own[:1] + expand_in + stream_in_own[1:] + project_in:
        cp.start()

    barrier = pltpu.get_barrier_semaphore()

    def greet(d, _):
        pl.semaphore_signal(barrier, inc=1, device_id=(lax.rem(i + d, 16), j), device_id_type=MESH)
        pl.semaphore_signal(barrier, inc=1, device_id=(i, lax.rem(j + d, 16)), device_id_type=MESH)
        return 0

    lax.fori_loop(1, 16, greet, 0)
    pl.semaphore_signal(barrier, inc=1, device_id=w_peer, device_id_type=MESH)

    @pl.when(i != j)
    def _():
        pl.semaphore_signal(barrier, inc=1, device_id=(j, i), device_id_type=MESH)

    for k in range(2):
        for h in range(2):
            stat_in[k * 2 + h].wait()
            v = sc[k, h].astype(F32)
            for n, col in enumerate((v, v * v)):
                total = jnp.sum(col, axis=1, keepdims=True)
                at_row = h * 4 + k * 2 + n
                st1[at_row : at_row + 1, :] = jnp.broadcast_to(total, (TOK, TOK)).T[0:1, :]
    r1[0] = st1[...]

    @pl.when(i != j)
    def _():
        pl.semaphore_wait(barrier, 32)

    @pl.when(i == j)
    def _():
        pl.semaphore_wait(barrier, 31)

    sent, ends = [], []

    def drain():
        for cp in sent:
            cp.wait_send()
        for end in ends:
            end()

    def start(cp):
        cp.start()
        sent.append(cp)
        return cp

    def nth_chunk(n):
        return lax.rem(z + 4 + (1 - 2 * lax.rem(n, 2)) * lax.div(n + 1, 2) + 8, 8)

    half_rows = pl.ds(pl.multiple_of(c * 64, 64), 64)

    def stream_copy(k, n):
        r = nth_chunk(n)
        rows = pl.multiple_of(((1 - xl) * 8 + r) * TOK + c * 64, 64)
        return copy(
            streams[k].at[pl.ds(rows, 64)], xs.at[k, r, half_rows], S_STREAM[k] + n, w_peer
        )

    def stream_forward(k, n):
        piece = xs.at[k, nth_chunk(n), half_rows]
        return copy(piece, piece, S_STREAM[k] + 8 + n, c_peer)

    def cols(h):
        return slice(h * W, (h + 1) * W)

    exp_cp = [
        [copy(expands[k].at[:, cols(h)], xe.at[k, h], S_EXP[k] + h, x_peer) for h in range(2)]
        for k in range(2)
    ]
    prj_cp = [copy(projects[k], xp.at[k], S_PROJ[k], x_peer) for k in range(2)]
    gain_cp = [copy(gains[k], xg[k], S_GAIN[k], x_peer) for k in range(2)]
    mine = pl.ds(pl.multiple_of(j * TOK, TOK), TOK)

    def stat1(d):
        return copy(st1, r1.at[d], S_STAT1 + d, (lax.rem(i + d, 16), j))

    def stat2(d):
        return copy(st2, r2.at[share], S_STAT2 + d, (i, xh * 8 + lax.rem(share + d, 8)))

    def run(fn, lo=1, hi=16):
        def body(d, _):
            fn(d)
            return 0

        lax.fori_loop(lo, hi, body, 0)

    run(lambda d: stat1(d).start())
    ends.append(lambda: run(lambda d: stat1(d).wait_send()))
    start(gain_cp[0])
    start(gain_cp[1])
    start(exp_cp[0][0])
    run(lambda n: stream_copy(0, n).start(), 0, 8)
    start(exp_cp[0][1])
    run(lambda d: stat1(d).wait_recv())
    totals = r1[0]
    for d in range(1, 16):
        totals = totals + r1[d]
    totals = totals * (1.0 / 6144.0)
    totals = jnp.where(xl == 0, totals[0:4, :], totals[4:8, :])
    st2[...] = jnp.zeros((8, TOK), F32)
    for k in range(2):
        mean = totals[2 * k : 2 * k + 1, :]
        var = totals[2 * k + 1 : 2 * k + 2, :] - mean * mean
        st2[2 * k : 2 * k + 1, :] = mean
        st2[2 * k + 1 : 2 * k + 2, :] = lax.rsqrt(var + EPS)
    r2[share] = st2[...]
    run(lambda d: stat2(d).start(), 1, 8)
    ends.append(lambda: run(lambda d: stat2(d).wait_send(), 1, 8))
    run(lambda d: stat2(d).wait_recv(), 1, 8)

    def normalise(k, part, r):
        t = xl * 8 + r
        stats = r2[r]
        mean = spread(stats[2 * k : 2 * k + 1, :])
        rstd = spread(stats[2 * k + 1 : 2 * k + 2, :])
        if part == 0:
            v = sv[k, pl.ds(pl.multiple_of(t * TOK, TOK), TOK), :]
            gain = gains[k][...]
        else:
            v = xs[k, r]
            gain = xg[k][...]
        mean, rstd = (jnp.concatenate([q, q, q], axis=1) for q in (mean, rstd))
        nrm[k, r, part] = ((v.astype(F32) - mean) * rstd * gain.reshape(1, W)).astype(BF16)

    def pass_on(k, lo, hi):
        def one(n):
            stream_copy(k, n).wait_recv()
            stream_forward(k, n).start()

        run(one, lo, hi)

    def prepare(k, lo, hi):
        def one(n):
            stream_forward(k, n).wait_recv()
            normalise(k, 1, nth_chunk(n))

        run(one, lo, hi)

    def partial_pre(k, r, h):
        own = jnp.dot(nrm[k, r, 0], ev[k, :, cols(h)], preferred_element_type=F32)
        return own + jnp.dot(nrm[k, r, 1], xe[k, h], preferred_element_type=F32)

    def rs_copy(k, s, way, half):
        sem = S_RS[k] + 4 * s + 2 * way + half
        return copy(rsb.at[k, s, way, half], rr.at[k, s, way, half], sem, (z_next, z_prev)[way])

    def rs_step(k, s, half):
        for way in range(2):
            if s == 0 and half != way:
                continue
            r = lax.rem(z + 4 - s + 8, 8) if way == 0 else lax.rem(z + 4 + s, 8)
            acc = partial_pre(k, r, half)
            if s > 1 or (s == 1 and half == way):
                rs_copy(k, s - 1, way, half).wait_recv()
                acc = acc + rr[k, s - 1, way, half].astype(F32)
            rsb[k, s, way, half] = acc.astype(BF16)
            rs_copy(k, s, way, half).start()

    def rs_sent(k):
        for way in range(2):
            rs_copy(k, 0, way, way).wait_send()
            for half in range(2):
                run(lambda s: rs_copy(k, s, way, half).wait_send(), 1, 4)

    def rs_finish(k):
        for half in range(2):
            acc = partial_pre(k, z, half) + shifts[k][cols(half)].reshape(1, W)
            for way in range(2):
                rs_copy(k, 3, way, half).wait_recv()
                acc = acc + rr[k, 3, way, half].astype(F32)
            act[k, z, half] = (0.5 * acc * (1.0 + lax.erf(acc * (0.5 ** 0.5)))).astype(BF16)

    def ag_copy(k, s, way, half):
        if way == 0:
            r, to = lax.rem(z - s + 8, 8), z_next
        else:
            r, to = lax.rem(z + s, 8), z_prev
        ref = act.at[k, r, half]
        return copy(ref, ref, S_AG[k] + 4 * s + 2 * way + half, to)

    def ag_step(k, s, first=False, last=False):
        for half in range(2):
            for way in range(2):
                if not first:
                    ag_copy(k, s - 1, way, half).wait_recv()
                if not last or half == way:
                    ag_copy(k, s, way, half).start()

    def ag_finish(k):
        for way in range(2):
            ag_copy(k, 3, way, way).wait_recv()

    def ag_sent(k):
        for way in range(2):
            for half in range(2):
                run(lambda s: ag_copy(k, s, way, half).wait_send(), 0, 3)
            ag_copy(k, 3, way, way).wait_send()

    def gemm2(k, r):
        for b, weight in enumerate((pv.at[k], xp.at[k])):
            out = jnp.dot(act[k, r, 0], weight[0:W, :], preferred_element_type=F32)
            out = out + jnp.dot(act[k, r, 1], weight[W:HID, :], preferred_element_type=F32)
            yb[k, lax.rem(r, 2), b, lax.div(r, 2)] = out.astype(BF16)

    def core_copy(k, b):
        return copy(yb.at[k, 1 - c, b], cr.at[k, b], S_CORE[k] + b, c_peer)

    def core_start(k):
        for b in (1, 0):
            start(core_copy(k, b))

    def y_copy(k, d, b):
        to = dev(xl, z, xh, lax.rem(y + d, 4), c)
        return copy(ys.at[k, d - 1, b], yr.at[k, d - 1, b], S_Y[k] + 2 * d + b, to)

    def chip_sum(k, t, b):
        return yb[k, c, b, t].astype(F32) + cr[k, b, t].astype(F32)

    def y_start(k):
        for b in (1, 0):
            core_copy(k, b).wait_recv()
            for d in (2, 1, 3):
                ys[k, d - 1, b] = chip_sum(k, lax.rem(y + d, 4), b).astype(BF16)
                start(y_copy(k, d, b))

    def x_copy_a(k):
        return copy(
            xt.at[k, 1], xr.at[k, xh], S_X[k], dev(1 - xl, z, xl, y, c), S_X[k] + xh
        )

    def x_copy_a_in(k, n):
        return copy(xt.at[k, 1], xr.at[k, n], S_X[k], x_peer, S_X[k] + n)

    def x_copy_b(k):
        return copy(xt.at[k, 0], xr.at[k, 2], S_X[k] + 2, dev(xl, z, 1 - xh, y, c))

    def x_start(k):
        for b in (1, 0):
            total = chip_sum(k, y, b)
            for d in (1, 3, 2):
                y_copy(k, d, b).wait_recv()
                total = total + yr[k, d - 1, b].astype(F32)
            xt[k, b] = total.astype(BF16)
            if b == 1:
                start(x_copy_a(k))
            else:

                @pl.when(xh != xl)
                def _():
                    x_copy_b(k).start()

    def finish(k):
        def put(branch):
            resid = sv[k, mine, :].astype(F32) + offsets[k][...].reshape(1, W)
            afters[k][...] = (resid + branch).astype(BF16)

        @pl.when(xh != xl)
        def _():
            x_copy_a_in(k, 0).wait_recv()
            x_copy_a_in(k, 1).wait_recv()
            put(xr[k, 0].astype(F32) + xr[k, 1].astype(F32))
            x_copy_b(k).wait_send()

        @pl.when(xh == xl)
        def _():
            x_copy_b(k).wait_recv()
            put(xt[k, 0].astype(F32) + xr[k, 2].astype(F32))

    gain_cp[0].wait_recv()
    gain_cp[1].wait_recv()
    stream_in_own[0].wait()
    expand_in[0].wait()
    pass_on(0, 0, 3)
    run(lambda r: normalise(0, 0, r), 0, 8)
    prepare(0, 0, 3)
    exp_cp[0][0].wait_recv()
    rs_step(0, 0, 0)
    pass_on(0, 3, 8)
    run(lambda n: stream_copy(1, n).start(), 0, 8)
    rs_step(0, 1, 0)
    prepare(0, 3, 5)
    exp_cp[0][1].wait_recv()
    start(exp_cp[1][0])
    start(exp_cp[1][1])
    rs_step(0, 0, 1)
    rs_step(0, 2, 0)
    prepare(0, 5, 8)
    rs_step(0, 1, 1)
    rs_step(0, 3, 0)
    stream_in_own[1].wait()
    run(lambda r: normalise(1, 0, r), 0, 8)
    rs_step(0, 2, 1)
    pass_on(1, 0, 8)
    rs_step(0, 3, 1)
    prepare(1, 0, 8)
    for k in range(2):
        ends.append(lambda k=k: run(lambda n: stream_copy(k, n).wait_send(), 0, 8))
        ends.append(lambda k=k: run(lambda n: stream_forward(k, n).wait_send(), 0, 8))
    ends.append(lambda: rs_sent(0))

    rs_finish(0)
    ag_step(0, 0, True)
    expand_in[1].wait()
    exp_cp[1][0].wait_recv()
    rs_step(1, 0, 0)
    exp_cp[1][1].wait_recv()
    start(prj_cp[0])
    rs_step(1, 0, 1)
    ag_step(0, 1)
    ag_step(0, 2)
    rs_step(1, 1, 0)
    rs_step(1, 1, 1)
    ag_step(0, 3, last=True)
    rs_step(1, 2, 0)
    rs_step(1, 2, 1)

    def gemm2_pair(k, s):
        gemm2(k, lax.rem(z - s + 8, 8))
        gemm2(k, lax.rem(z + s, 8))

    project_in[0].wait()
    project_in[1].wait()
    prj_cp[0].wait_recv()
    start(prj_cp[1])
    gemm2(0, z)
    gemm2_pair(0, 1)
    gemm2_pair(0, 2)
    rs_step(1, 3, 0)
    rs_step(1, 3, 1)
    ag_finish(0)
    gemm2_pair(0, 3)
    gemm2(0, lax.rem(z + 4, 8))
    core_start(0)
    ends.append(lambda: rs_sent(1))
    ends.append(lambda: ag_sent(0))
    rs_finish(1)

    place = xh * 4 + y

    def left_copy(d):
        to = lax.rem(place + d, 8)
        return copy(a_l, al.at[share, xh], S_LEFT + d, (i, to * 2 + c))

    def left_forward(d):
        came = lax.rem(place - d + 8, 8)
        ref = al.at[lax.rem(came, 4) * 2 + c, lax.div(came, 4)]
        return copy(ref, ref, S_LEFTC + d, c_peer)

    def left_pass(d):
        left_copy(d).wait_recv()
        left_forward(d).start()

    ag_step(1, 0, True)
    y_start(0)
    ag_step(1, 1)
    prj_cp[1].wait_recv()
    gemm2(1, z)
    gemm2_pair(1, 1)
    x_start(0)
    ag_step(1, 2)
    gemm2_pair(1, 2)
    finish(0)
    al[share, xh] = a_l[...]
    run(lambda d: left_copy(d).start(), 1, 8)
    left_forward(0).start()
    ends.append(lambda: run(lambda d: left_copy(d).wait_send(), 1, 8))
    ends.append(lambda: run(lambda d: left_forward(d).wait_send(), 0, 8))
    ag_step(1, 3, last=True)
    gemm2_pair(1, 3)
    ag_finish(1)
    ends.append(lambda: ag_sent(1))
    gemm2(1, lax.rem(z + 4, 8))
    core_start(1)
    y_start(1)
    run(left_pass, 1, 8)
    x_start(1)
    finish(1)

    turn = copy(a_r, at.at[lax.rem(j, 8), lax.div(j, 8)], S_TURN, (j, i))

    @pl.when(i != j)
    def _():
        turn.start()

    @pl.when(i == j)
    def _():
        at[z, xl] = a_r[...]

    @pl.when(i != j)
    def _():
        turn.wait()

    here = at.at[z, xl]
    pair = start(copy(here, here, S_PAIR, x_peer))

    def right_copy(s, way, which):
        if way == 0:
            r, to = lax.rem(z - s + 8, 8), z_next
        else:
            r, to = lax.rem(z + s, 8), z_prev
        ref = at.at[r, xl if which == 0 else 1 - xl]
        return copy(ref, ref, S_RIGHT + 4 * s + 2 * way + which, to)

    def add(r, first=False):
        term = lax.dot_general(
            al[r].reshape(2 * TOK, W),
            at[r].reshape(2 * TOK, W),
            (((0,), (0,)), ((), ())),
            preferred_element_type=F32,
        )
        corr[...] = term if first else corr[...] + term

    def across(n):
        ref = at.at[lax.rem(z + (5, 3, 4)[n], 8), xl]
        return copy(ref, ref, S_CROSS + n, x_peer)

    def add_pair(s):
        add(lax.rem(z - s + 8, 8))
        add(lax.rem(z + s, 8))

    for way in range(2):
        start(right_copy(0, way, 0))
    pair.wait_recv()
    for way in range(2):
        start(right_copy(0, way, 1))
    for which in range(2):
        for way in range(2):
            right_copy(0, way, which).wait_recv()
            start(right_copy(1, way, which))
    for way in range(2):
        right_copy(1, way, 0).wait_recv()
        start(right_copy(2, way, 0))
    run(lambda d: left_forward(d).wait_recv(), 0, 8)
    add(z, True)
    add_pair(1)
    right_copy(2, 0, 0).wait_recv()
    start(right_copy(3, 0, 0))
    start(across(0))
    right_copy(2, 1, 0).wait_recv()
    start(across(1))
    for way in range(2):
        right_copy(1, way, 1).wait_recv()
    add_pair(2)
    right_copy(3, 0, 0).wait_recv()
    start(across(2))
    across(0).wait_recv()
    across(1).wait_recv()
    add_pair(3)
    across(2).wait_recv()
    add(lax.rem(z + 4, 8))
    drain()


def hand_out(a_l, a_r, corr, a_l_out, a_r_out, corr_out):
    a_l_out[...] = a_l[...]
    a_r_out[...] = a_r[...]
    corr_out[...] = corr[...] * (1.0 / 2048.0)


def per_device(s_l, s_r, g_l, g_r, e_l, e_r, b_l, b_r, p_l, p_r, o_l, o_r):
    vm = pl.BlockSpec(memory_space=pltpu.VMEM)
    hbm = pl.BlockSpec(memory_space=pl.ANY)
    tile = (TOK, W)
    shapes = (
        jax.ShapeDtypeStruct(tile, BF16),
        jax.ShapeDtypeStruct(tile, BF16),
        jax.ShapeDtypeStruct((W, W), F32),
    )
    results = pl.pallas_call(
        kernel,
        out_shape=shapes,
        in_specs=[hbm, hbm, vm, vm, hbm, hbm, vm, vm, hbm, hbm, vm, vm],
        out_specs=(vm, vm, vm),
        scratch_shapes=[
            pltpu.VMEM((8, TOK), F32),
            pltpu.VMEM((8, TOK), F32),
            pltpu.VMEM((16, 8, TOK), F32),
            pltpu.VMEM((8, 8, TOK), F32),
            pltpu.VMEM((2, 2, W, W), BF16),
            pltpu.VMEM((2, HID, W), BF16),
            pltpu.VMEM((W,), F32),
            pltpu.VMEM((W,), F32),
            pltpu.VMEM((2, 8) + tile, BF16),
            pltpu.VMEM((2, 8, 2) + tile, BF16),
            pltpu.VMEM((2, 4, 2, 2) + tile, BF16),
            pltpu.VMEM((2, 4, 2, 2) + tile, BF16),
            pltpu.VMEM((2, 8, 2) + tile, BF16),
            pltpu.VMEM((2, 2, 2, 4) + tile, BF16),
            pltpu.VMEM((2, 2, 4) + tile, BF16),
            pltpu.VMEM((2, 3, 2) + tile, BF16),
            pltpu.VMEM((2, 3, 2) + tile, BF16),
            pltpu.VMEM((2, 2) + tile, BF16),
            pltpu.VMEM((2, 3) + tile, BF16),
            pltpu.VMEM((8, 2) + tile, BF16),
            pltpu.VMEM((8, 2) + tile, BF16),
            pltpu.VMEM((2, 2) + tile, BF16),
            pltpu.VMEM((2, 2048, W), BF16),
            pltpu.VMEM((2, W, HID), BF16),
            pltpu.VMEM((2, HID, W), BF16),
            pltpu.SemaphoreType.DMA((N_SEMS,)),
            pltpu.SemaphoreType.DMA((N_SEMS,)),
            pltpu.SemaphoreType.DMA((10,)),
        ],
        compiler_params=pltpu.CompilerParams(
            collective_id=0, has_side_effects=True, vmem_limit_bytes=56 * 1024 * 1024
        ),
    )(s_l, s_r, g_l, g_r, e_l, e_r, b_l, b_r, p_l, p_r, o_l, o_r)
    return pl.pallas_call(
        hand_out,
        out_shape=shapes,
        in_specs=[vm] * 3,
        out_specs=(vm,) * 3,
    )(*results)


def solution(mesh):
    placed = (
        P(None, "dp"),
        P(None, "dp"),
        P("dp"),
        P("dp"),
        P("dp", "mp"),
        P("dp", "mp"),
        P("mp"),
        P("mp"),
        P("mp", "dp"),
        P("mp", "dp"),
        P("dp"),
        P("dp"),
    )
    return jax.shard_map(
        per_device,
        mesh=mesh,
        in_specs=placed,
        out_specs=(P("mp", "dp"), P("mp", "dp"), P("dp", "mp")),
        check_vma=False,
    )
```

```python
import functools

import jax
import jax.numpy as jnp
from jax import lax
from jax.experimental import pallas as pl
from jax.experimental.pallas import tpu as pltpu
from jax.sharding import PartitionSpec as P

EPS = 1e-06
F32 = jnp.float32
BF16 = jnp.bfloat16
MESH = pl.DeviceIdType.MESH

NZ, NY = 8, 4
TOK = 128
W = 384
HID = 768


class Slots:
    def __init__(self):
        self.count = 0

    def take(self, n):
        first = self.count
        self.count += n
        return first


SLOTS = Slots()
S_STAT1 = SLOTS.take(16)
S_STAT2 = SLOTS.take(16)
S_EXP = [SLOTS.take(2) for _ in range(2)]
S_PROJ = [SLOTS.take(1) for _ in range(2)]
S_GAIN = [SLOTS.take(1) for _ in range(2)]
S_STREAM = [SLOTS.take(16) for _ in range(2)]
S_RS = [SLOTS.take(32) for _ in range(2)]
S_AG = [SLOTS.take(32) for _ in range(2)]
S_CORE = [SLOTS.take(2) for _ in range(2)]
S_Y = [SLOTS.take(8) for _ in range(2)]
S_X = [SLOTS.take(3) for _ in range(2)]
S_LEFT = SLOTS.take(8)
S_LEFTC = SLOTS.take(8)
S_TURN = SLOTS.take(2)
S_PAIR = SLOTS.take(2)
S_RIGHT = SLOTS.take(32)
S_CROSS = SLOTS.take(6)
N_SEMS = SLOTS.count


def spread(row, size=TOK):
    return jnp.broadcast_to(row, (size, size)).T


def kernel(
    s_l, s_r, g_l, g_r, e_l, e_r, b_l, b_r, p_l, p_r, o_l, o_r,
    a_l, a_r, corr,
    st1, st2, r1, r2, xe, xp, xg0, xg1, xs, nrm, rr, rsb, act, yb, cr, ys, yr, xt, xr, al, at,
    sc, sv, ev, pv, ssem, rsem, lsem,
):
    streams, gains, expands, shifts = (s_l, s_r), (g_l, g_r), (e_l, e_r), (b_l, b_r)
    projects, offsets, afters, xg = (p_l, p_r), (o_l, o_r), (a_l, a_r), (xg0, xg1)
    i, j = lax.axis_index("dp"), lax.axis_index("mp")
    xl, z = lax.div(i, 8), lax.rem(i, 8)
    xh, y, c = lax.div(j, 8), lax.rem(lax.div(j, 2), 4), lax.rem(j, 2)

    def dev(xl_, z_, xh_, y_, c_):
        return (xl_ * 8 + z_, xh_ * 8 + y_ * 2 + c_)

    def copy(src, dst, sem, to, rsem_at=None):
        return pltpu.make_async_remote_copy(
            src_ref=src,
            dst_ref=dst,
            send_sem=ssem.at[sem],
            recv_sem=rsem.at[sem if rsem_at is None else rsem_at],
            device_id=to,
            device_id_type=MESH,
        )

    x_peer = dev(1 - xl, z, xh, y, c)
    w_peer = dev(1 - xl, z, 1 - xh, y, c)
    c_peer = dev(xl, z, xh, y, 1 - c)
    z_next = dev(xl, lax.rem(z + 1, 8), xh, y, c)
    z_prev = dev(xl, lax.rem(z + 7, 8), xh, y, c)

    share = y * 2 + c

    def token_rows(h):
        return pl.ds(pl.multiple_of((h * 8 + share) * TOK, TOK), TOK)

    stat_in = [
        pltpu.make_async_copy(streams[k].at[token_rows(h)], sc.at[k, h], lsem.at[k * 2 + h])
        for k in range(2)
        for h in range(2)
    ]
    stream_in_own = [pltpu.make_async_copy(streams[k], sv.at[k], lsem.at[4 + k]) for k in range(2)]
    expand_in = [pltpu.make_async_copy(expands[k], ev.at[k], lsem.at[6 + k]) for k in range(2)]
    project_in = [pltpu.make_async_copy(projects[k], pv.at[k], lsem.at[8 + k]) for k in range(2)]
    for cp in stat_in + stream_in_own[:1] + expand_in + stream_in_own[1:] + project_in:
        cp.start()

    barrier = pltpu.get_barrier_semaphore()

    def greet(d, _):
        pl.semaphore_signal(barrier, inc=1, device_id=(lax.rem(i + d, 16), j), device_id_type=MESH)
        pl.semaphore_signal(barrier, inc=1, device_id=(i, lax.rem(j + d, 16)), device_id_type=MESH)
        return 0

    lax.fori_loop(1, 16, greet, 0)
    pl.semaphore_signal(barrier, inc=1, device_id=w_peer, device_id_type=MESH)

    @pl.when(i != j)
    def _():
        pl.semaphore_signal(barrier, inc=1, device_id=(j, i), device_id_type=MESH)

    for k in range(2):
        for h in range(2):
            stat_in[k * 2 + h].wait()
            v = sc[k, h].astype(F32)
            for n, col in enumerate((v, v * v)):
                total = jnp.sum(col, axis=1, keepdims=True)
                at_row = h * 4 + k * 2 + n
                st1[at_row : at_row + 1, :] = jnp.broadcast_to(total, (TOK, TOK)).T[0:1, :]
    r1[0] = st1[...]

    @pl.when(i != j)
    def _():
        pl.semaphore_wait(barrier, 32)

    @pl.when(i == j)
    def _():
        pl.semaphore_wait(barrier, 31)

    sent, ends = [], []

    def drain():
        for cp in sent:
            cp.wait_send()
        for end in ends:
            end()

    def start(cp):
        cp.start()
        sent.append(cp)
        return cp

    def nth_chunk(n):
        return lax.rem(z + 4 + (1 - 2 * lax.rem(n, 2)) * lax.div(n + 1, 2) + 8, 8)

    half_rows = pl.ds(pl.multiple_of(c * 64, 64), 64)

    def stream_copy(k, n):
        r = nth_chunk(n)
        rows = pl.multiple_of(((1 - xl) * 8 + r) * TOK + c * 64, 64)
        return copy(
            streams[k].at[pl.ds(rows, 64)], xs.at[k, r, half_rows], S_STREAM[k] + n, w_peer
        )

    def stream_forward(k, n):
        piece = xs.at[k, nth_chunk(n), half_rows]
        return copy(piece, piece, S_STREAM[k] + 8 + n, c_peer)

    def cols(h):
        return slice(h * W, (h + 1) * W)

    exp_cp = [
        [copy(expands[k].at[:, cols(h)], xe.at[k, h], S_EXP[k] + h, x_peer) for h in range(2)]
        for k in range(2)
    ]
    prj_cp = [copy(projects[k], xp.at[k], S_PROJ[k], x_peer) for k in range(2)]
    gain_cp = [copy(gains[k], xg[k], S_GAIN[k], x_peer) for k in range(2)]
    mine = pl.ds(pl.multiple_of(j * TOK, TOK), TOK)

    def stat1(d):
        return copy(st1, r1.at[d], S_STAT1 + d, (lax.rem(i + d, 16), j))

    def stat2(d):
        return copy(st2, r2.at[share], S_STAT2 + d, (i, xh * 8 + lax.rem(share + d, 8)))

    def run(fn, lo=1, hi=16):
        def body(d, _):
            fn(d)
            return 0

        lax.fori_loop(lo, hi, body, 0)

    run(lambda d: stat1(d).start())
    ends.append(lambda: run(lambda d: stat1(d).wait_send()))
    start(gain_cp[0])
    start(gain_cp[1])
    start(exp_cp[0][0])
    run(lambda n: stream_copy(0, n).start(), 0, 8)
    start(exp_cp[0][1])
    run(lambda d: stat1(d).wait_recv())
    totals = r1[0]
    for d in range(1, 16):
        totals = totals + r1[d]
    totals = totals * (1.0 / 6144.0)
    totals = jnp.where(xl == 0, totals[0:4, :], totals[4:8, :])
    st2[...] = jnp.zeros((8, TOK), F32)
    for k in range(2):
        mean = totals[2 * k : 2 * k + 1, :]
        var = totals[2 * k + 1 : 2 * k + 2, :] - mean * mean
        st2[2 * k : 2 * k + 1, :] = mean
        st2[2 * k + 1 : 2 * k + 2, :] = lax.rsqrt(var + EPS)
    r2[share] = st2[...]
    run(lambda d: stat2(d).start(), 1, 8)
    ends.append(lambda: run(lambda d: stat2(d).wait_send(), 1, 8))
    run(lambda d: stat2(d).wait_recv(), 1, 8)

    def normalise(k, part, r):
        t = xl * 8 + r
        stats = r2[r]
        mean = spread(stats[2 * k : 2 * k + 1, :])
        rstd = spread(stats[2 * k + 1 : 2 * k + 2, :])
        if part == 0:
            v = sv[k, pl.ds(pl.multiple_of(t * TOK, TOK), TOK), :]
            gain = gains[k][...]
        else:
            v = xs[k, r]
            gain = xg[k][...]
        mean, rstd = (jnp.concatenate([q, q, q], axis=1) for q in (mean, rstd))
        nrm[k, r, part] = ((v.astype(F32) - mean) * rstd * gain.reshape(1, W)).astype(BF16)

    def pass_on(k, lo, hi):
        def one(n):
            stream_copy(k, n).wait_recv()
            stream_forward(k, n).start()

        run(one, lo, hi)

    def prepare(k, lo, hi):
        def one(n):
            stream_forward(k, n).wait_recv()
            normalise(k, 1, nth_chunk(n))

        run(one, lo, hi)

    def partial_pre(k, r, h):
        own = jnp.dot(nrm[k, r, 0], ev[k, :, cols(h)], preferred_element_type=F32)
        return own + jnp.dot(nrm[k, r, 1], xe[k, h], preferred_element_type=F32)

    def piece(ref, u):
        return ref.at[pl.ds(u * 64, 64)]

    def rs_copy(k, s, way, half, u):
        sem = S_RS[k] + 8 * s + 4 * way + 2 * half + u
        src, dst = rsb.at[k, s, way, half], rr.at[k, s, way, half]
        return copy(piece(src, u), piece(dst, u), sem, (z_next, z_prev)[way])

    def rs_step(k, s, half):
        ways = [way for way in range(2) if s > 0 or half == way]
        own = {}
        for way in ways:
            r = lax.rem(z + 4 - s + 8, 8) if way == 0 else lax.rem(z + 4 + s, 8)
            own[way] = partial_pre(k, r, half)
        for u in range(2):
            rows = slice(u * 64, (u + 1) * 64)
            for way in ways:
                acc = own[way][rows]
                if s > 1 or (s == 1 and half == way):
                    rs_copy(k, s - 1, way, half, u).wait_recv()
                    acc = acc + rr[k, s - 1, way, half, rows].astype(F32)
                rsb[k, s, way, half, rows] = acc.astype(BF16)
                rs_copy(k, s, way, half, u).start()

    def rs_sent(k):
        for u in range(2):
            for way in range(2):
                rs_copy(k, 0, way, way, u).wait_send()
                for half in range(2):
                    run(lambda s: rs_copy(k, s, way, half, u).wait_send(), 1, 4)

    def rs_finish(k):
        for half in range(2):
            acc = partial_pre(k, z, half) + shifts[k][cols(half)].reshape(1, W)
            for way in range(2):
                for u in range(2):
                    rs_copy(k, 3, way, half, u).wait_recv()
                acc = acc + rr[k, 3, way, half].astype(F32)
            act[k, z, half] = (0.5 * acc * (1.0 + lax.erf(acc * (0.5 ** 0.5)))).astype(BF16)

    def ag_copy(k, s, way, half, u):
        if way == 0:
            r, to = lax.rem(z - s + 8, 8), z_next
        else:
            r, to = lax.rem(z + s, 8), z_prev
        ref = piece(act.at[k, r, half], u)
        return copy(ref, ref, S_AG[k] + 8 * s + 4 * way + 2 * half + u, to)

    def ag_step(k, s, first=False, last=False):
        for half in range(2):
            for u in range(2):
                for way in range(2):
                    if not first:
                        ag_copy(k, s - 1, way, half, u).wait_recv()
                    if not last or half == way:
                        ag_copy(k, s, way, half, u).start()

    def ag_finish(k):
        for u in range(2):
            for way in range(2):
                ag_copy(k, 3, way, way, u).wait_recv()

    def ag_sent(k):
        for u in range(2):
            for way in range(2):
                for half in range(2):
                    run(lambda s: ag_copy(k, s, way, half, u).wait_send(), 0, 3)
                ag_copy(k, 3, way, way, u).wait_send()

    def gemm2(k, r):
        for b, weight in enumerate((pv.at[k], xp.at[k])):
            out = jnp.dot(act[k, r, 0], weight[0:W, :], preferred_element_type=F32)
            out = out + jnp.dot(act[k, r, 1], weight[W:HID, :], preferred_element_type=F32)
            yb[k, lax.rem(r, 2), b, lax.div(r, 2)] = out.astype(BF16)

    def core_copy(k, b):
        return copy(yb.at[k, 1 - c, b], cr.at[k, b], S_CORE[k] + b, c_peer)

    def core_start(k):
        for b in (1, 0):
            start(core_copy(k, b))

    def y_copy(k, d, b):
        to = dev(xl, z, xh, lax.rem(y + d, 4), c)
        return copy(ys.at[k, d - 1, b], yr.at[k, d - 1, b], S_Y[k] + 2 * d + b, to)

    def chip_sum(k, t, b):
        return yb[k, c, b, t].astype(F32) + cr[k, b, t].astype(F32)

    def y_start(k):
        for b in (1, 0):
            core_copy(k, b).wait_recv()
            for d in (2, 1, 3):
                ys[k, d - 1, b] = chip_sum(k, lax.rem(y + d, 4), b).astype(BF16)
                start(y_copy(k, d, b))

    def x_copy_a(k):
        return copy(
            xt.at[k, 1], xr.at[k, xh], S_X[k], dev(1 - xl, z, xl, y, c), S_X[k] + xh
        )

    def x_copy_a_in(k, n):
        return copy(xt.at[k, 1], xr.at[k, n], S_X[k], x_peer, S_X[k] + n)

    def x_copy_b(k):
        return copy(xt.at[k, 0], xr.at[k, 2], S_X[k] + 2, dev(xl, z, 1 - xh, y, c))

    def x_start(k):
        for b in (1, 0):
            total = chip_sum(k, y, b)
            for d in (1, 3, 2):
                y_copy(k, d, b).wait_recv()
                total = total + yr[k, d - 1, b].astype(F32)
            xt[k, b] = total.astype(BF16)
            if b == 1:
                start(x_copy_a(k))
            else:

                @pl.when(xh != xl)
                def _():
                    x_copy_b(k).start()

    def finish(k):
        def put(branch):
            resid = sv[k, mine, :].astype(F32) + offsets[k][...].reshape(1, W)
            afters[k][...] = (resid + branch).astype(BF16)

        @pl.when(xh != xl)
        def _():
            x_copy_a_in(k, 0).wait_recv()
            x_copy_a_in(k, 1).wait_recv()
            put(xr[k, 0].astype(F32) + xr[k, 1].astype(F32))
            x_copy_b(k).wait_send()

        @pl.when(xh == xl)
        def _():
            x_copy_b(k).wait_recv()
            put(xt[k, 0].astype(F32) + xr[k, 2].astype(F32))

    gain_cp[0].wait_recv()
    gain_cp[1].wait_recv()
    stream_in_own[0].wait()
    expand_in[0].wait()
    pass_on(0, 0, 3)
    run(lambda r: normalise(0, 0, r), 0, 8)
    prepare(0, 0, 3)
    exp_cp[0][0].wait_recv()
    rs_step(0, 0, 0)
    pass_on(0, 3, 8)
    run(lambda n: stream_copy(1, n).start(), 0, 8)
    rs_step(0, 1, 0)
    prepare(0, 3, 5)
    exp_cp[0][1].wait_recv()
    start(exp_cp[1][0])
    start(exp_cp[1][1])
    rs_step(0, 0, 1)
    rs_step(0, 2, 0)
    prepare(0, 5, 8)
    rs_step(0, 1, 1)
    rs_step(0, 3, 0)
    stream_in_own[1].wait()
    run(lambda r: normalise(1, 0, r), 0, 8)
    rs_step(0, 2, 1)
    pass_on(1, 0, 8)
    rs_step(0, 3, 1)
    prepare(1, 0, 8)
    for k in range(2):
        ends.append(lambda k=k: run(lambda n: stream_copy(k, n).wait_send(), 0, 8))
        ends.append(lambda k=k: run(lambda n: stream_forward(k, n).wait_send(), 0, 8))
    ends.append(lambda: rs_sent(0))

    expand_in[1].wait()
    exp_cp[1][0].wait_recv()
    rs_step(1, 0, 0)
    exp_cp[1][1].wait_recv()
    start(prj_cp[0])
    rs_step(1, 0, 1)
    rs_finish(0)
    ag_step(0, 0, True)
    ag_step(0, 1)
    ag_step(0, 2)
    rs_step(1, 1, 0)
    rs_step(1, 1, 1)
    ag_step(0, 3, last=True)
    rs_step(1, 2, 0)
    rs_step(1, 2, 1)

    def gemm2_pair(k, s):
        gemm2(k, lax.rem(z - s + 8, 8))
        gemm2(k, lax.rem(z + s, 8))

    project_in[0].wait()
    project_in[1].wait()
    prj_cp[0].wait_recv()
    start(prj_cp[1])
    gemm2(0, z)
    gemm2_pair(0, 1)
    gemm2_pair(0, 2)
    rs_step(1, 3, 0)
    rs_step(1, 3, 1)
    ag_finish(0)
    gemm2_pair(0, 3)
    gemm2(0, lax.rem(z + 4, 8))
    core_start(0)
    ends.append(lambda: rs_sent(1))
    ends.append(lambda: ag_sent(0))
    rs_finish(1)

    place = xh * 4 + y

    def left_copy(d):
        to = lax.rem(place + d, 8)
        return copy(a_l, al.at[share, xh], S_LEFT + d, (i, to * 2 + c))

    def left_forward(d):
        came = lax.rem(place - d + 8, 8)
        ref = al.at[lax.rem(came, 4) * 2 + c, lax.div(came, 4)]
        return copy(ref, ref, S_LEFTC + d, c_peer)

    def left_pass(d):
        left_copy(d).wait_recv()
        left_forward(d).start()

    ag_step(1, 0, True)
    y_start(0)
    ag_step(1, 1)
    prj_cp[1].wait_recv()
    gemm2(1, z)
    gemm2_pair(1, 1)
    ag_step(1, 2)
    gemm2_pair(1, 2)
    x_start(0)
    ag_step(1, 3, last=True)
    gemm2_pair(1, 3)
    finish(0)
    al[share, xh] = a_l[...]
    run(lambda d: left_copy(d).start(), 1, 8)
    left_forward(0).start()
    ends.append(lambda: run(lambda d: left_copy(d).wait_send(), 1, 8))
    ends.append(lambda: run(lambda d: left_forward(d).wait_send(), 0, 8))
    ag_finish(1)
    ends.append(lambda: ag_sent(1))
    gemm2(1, lax.rem(z + 4, 8))
    core_start(1)
    y_start(1)
    run(left_pass, 1, 8)
    x_start(1)
    finish(1)

    def turn(u):
        there = piece(at.at[lax.rem(j, 8), lax.div(j, 8)], u)
        return copy(piece(a_r, u), there, S_TURN + u, (j, i))

    @pl.when(i != j)
    def _():
        turn(0).start()
        turn(1).start()

    @pl.when(i == j)
    def _():
        at[z, xl] = a_r[...]

    def pair(u):
        here = piece(at.at[z, xl], u)
        return copy(here, here, S_PAIR + u, x_peer)

    def right_copy(s, way, which, u):
        if way == 0:
            r, to = lax.rem(z - s + 8, 8), z_next
        else:
            r, to = lax.rem(z + s, 8), z_prev
        ref = piece(at.at[r, xl if which == 0 else 1 - xl], u)
        return copy(ref, ref, S_RIGHT + 8 * s + 4 * way + 2 * which + u, to)

    def add(r, first=False):
        term = lax.dot_general(
            al[r].reshape(2 * TOK, W),
            at[r].reshape(2 * TOK, W),
            (((0,), (0,)), ((), ())),
            preferred_element_type=F32,
        )
        corr[...] = term if first else corr[...] + term

    def across(n, u):
        ref = piece(at.at[lax.rem(z + (5, 3, 4)[n], 8), xl], u)
        return copy(ref, ref, S_CROSS + 2 * n + u, x_peer)

    def add_pair(s):
        add(lax.rem(z - s + 8, 8))
        add(lax.rem(z + s, 8))

    for u in range(2):

        @pl.when(i != j)
        def _(u=u):
            turn(u).wait_recv()

        for way in range(2):
            start(right_copy(0, way, 0, u))
        start(pair(u))
    for u in range(2):
        pair(u).wait_recv()
        for way in range(2):
            start(right_copy(0, way, 1, u))
    for s, which in ((1, 0), (1, 1), (2, 0)):
        for u in range(2):
            for way in range(2):
                right_copy(s - 1, way, which, u).wait_recv()
                start(right_copy(s, way, which, u))
    run(lambda d: left_forward(d).wait_recv(), 0, 8)
    add(z, True)
    add_pair(1)
    for u in range(2):
        right_copy(2, 0, 0, u).wait_recv()
        start(right_copy(3, 0, 0, u))
        start(across(0, u))
        right_copy(2, 1, 0, u).wait_recv()
        start(across(1, u))
    for u in range(2):
        for way in range(2):
            right_copy(1, way, 1, u).wait_recv()
    add_pair(2)
    for u in range(2):
        right_copy(3, 0, 0, u).wait_recv()
        start(across(2, u))
    for n in range(2):
        for u in range(2):
            across(n, u).wait_recv()
    add_pair(3)
    for u in range(2):
        across(2, u).wait_recv()
    add(lax.rem(z + 4, 8))

    @pl.when(i != j)
    def _():
        turn(0).wait_send()
        turn(1).wait_send()

    drain()


def hand_out(a_l, a_r, corr, a_l_out, a_r_out, corr_out):
    a_l_out[...] = a_l[...]
    a_r_out[...] = a_r[...]
    corr_out[...] = corr[...] * (1.0 / 2048.0)


def per_device(s_l, s_r, g_l, g_r, e_l, e_r, b_l, b_r, p_l, p_r, o_l, o_r):
    vm = pl.BlockSpec(memory_space=pltpu.VMEM)
    hbm = pl.BlockSpec(memory_space=pl.ANY)
    tile = (TOK, W)
    shapes = (
        jax.ShapeDtypeStruct(tile, BF16),
        jax.ShapeDtypeStruct(tile, BF16),
        jax.ShapeDtypeStruct((W, W), F32),
    )
    results = pl.pallas_call(
        kernel,
        out_shape=shapes,
        in_specs=[hbm, hbm, vm, vm, hbm, hbm, vm, vm, hbm, hbm, vm, vm],
        out_specs=(vm, vm, vm),
        scratch_shapes=[
            pltpu.VMEM((8, TOK), F32),
            pltpu.VMEM((8, TOK), F32),
            pltpu.VMEM((16, 8, TOK), F32),
            pltpu.VMEM((8, 8, TOK), F32),
            pltpu.VMEM((2, 2, W, W), BF16),
            pltpu.VMEM((2, HID, W), BF16),
            pltpu.VMEM((W,), F32),
            pltpu.VMEM((W,), F32),
            pltpu.VMEM((2, 8) + tile, BF16),
            pltpu.VMEM((2, 8, 2) + tile, BF16),
            pltpu.VMEM((2, 4, 2, 2) + tile, BF16),
            pltpu.VMEM((2, 4, 2, 2) + tile, BF16),
            pltpu.VMEM((2, 8, 2) + tile, BF16),
            pltpu.VMEM((2, 2, 2, 4) + tile, BF16),
            pltpu.VMEM((2, 2, 4) + tile, BF16),
            pltpu.VMEM((2, 3, 2) + tile, BF16),
            pltpu.VMEM((2, 3, 2) + tile, BF16),
            pltpu.VMEM((2, 2) + tile, BF16),
            pltpu.VMEM((2, 3) + tile, BF16),
            pltpu.VMEM((8, 2) + tile, BF16),
            pltpu.VMEM((8, 2) + tile, BF16),
            pltpu.VMEM((2, 2) + tile, BF16),
            pltpu.VMEM((2, 2048, W), BF16),
            pltpu.VMEM((2, W, HID), BF16),
            pltpu.VMEM((2, HID, W), BF16),
            pltpu.SemaphoreType.DMA((N_SEMS,)),
            pltpu.SemaphoreType.DMA((N_SEMS,)),
            pltpu.SemaphoreType.DMA((10,)),
        ],
        compiler_params=pltpu.CompilerParams(
            collective_id=0, has_side_effects=True, vmem_limit_bytes=56 * 1024 * 1024
        ),
    )(s_l, s_r, g_l, g_r, e_l, e_r, b_l, b_r, p_l, p_r, o_l, o_r)
    return pl.pallas_call(
        hand_out,
        out_shape=shapes,
        in_specs=[vm] * 3,
        out_specs=(vm,) * 3,
    )(*results)


def solution(mesh):
    placed = (
        P(None, "dp"),
        P(None, "dp"),
        P("dp"),
        P("dp"),
        P("dp", "mp"),
        P("dp", "mp"),
        P("mp"),
        P("mp"),
        P("mp", "dp"),
        P("mp", "dp"),
        P("dp"),
        P("dp"),
    )
    return jax.shard_map(
        per_device,
        mesh=mesh,
        in_specs=placed,
        out_specs=(P("mp", "dp"), P("mp", "dp"), P("dp", "mp")),
        check_vma=False,
    )
```

```python
import functools

import jax
import jax.numpy as jnp
from jax import lax
from jax.experimental import pallas as pl
from jax.experimental.pallas import tpu as pltpu
from jax.sharding import PartitionSpec as P

EPS = 1e-06
F32 = jnp.float32
BF16 = jnp.bfloat16
MESH = pl.DeviceIdType.MESH

NZ, NY = 8, 4
TOK = 128
W = 384
HID = 768


class Slots:
    def __init__(self):
        self.count = 0

    def take(self, n):
        first = self.count
        self.count += n
        return first


SLOTS = Slots()
S_STAT1 = SLOTS.take(16)
S_STAT2 = SLOTS.take(16)
S_EXP = [SLOTS.take(2) for _ in range(2)]
S_PROJ = [SLOTS.take(1) for _ in range(2)]
S_GAIN = [SLOTS.take(1) for _ in range(2)]
S_STREAM = [SLOTS.take(16) for _ in range(2)]
S_RS = [SLOTS.take(32) for _ in range(2)]
S_AG = [SLOTS.take(32) for _ in range(2)]
S_CORE = [SLOTS.take(2) for _ in range(2)]
S_Y = [SLOTS.take(8) for _ in range(2)]
S_X = [SLOTS.take(3) for _ in range(2)]
S_LEFT = SLOTS.take(8)
S_LEFTC = SLOTS.take(8)
S_TURN = SLOTS.take(2)
S_PAIR = SLOTS.take(2)
S_RIGHT = SLOTS.take(32)
S_CROSS = SLOTS.take(6)
N_SEMS = SLOTS.count


def spread(row, size=TOK):
    return jnp.broadcast_to(row, (size, size)).T


def kernel(
    s_l, s_r, g_l, g_r, e_l, e_r, b_l, b_r, p_l, p_r, o_l, o_r,
    a_l, a_r, corr,
    st1, st2, r1, r2, xe, xp, xg0, xg1, xs, nrm, rr, rsb, act, yb, cr, ys, yr, xt, xr, al, at,
    sc, sv, ev, pv, ssem, rsem, lsem,
):
    streams, gains, expands, shifts = (s_l, s_r), (g_l, g_r), (e_l, e_r), (b_l, b_r)
    projects, offsets, afters, xg = (p_l, p_r), (o_l, o_r), (a_l, a_r), (xg0, xg1)
    i, j = lax.axis_index("dp"), lax.axis_index("mp")
    xl, z = lax.div(i, 8), lax.rem(i, 8)
    xh, y, c = lax.div(j, 8), lax.rem(lax.div(j, 2), 4), lax.rem(j, 2)

    def dev(xl_, z_, xh_, y_, c_):
        return (xl_ * 8 + z_, xh_ * 8 + y_ * 2 + c_)

    def copy(src, dst, sem, to, rsem_at=None):
        return pltpu.make_async_remote_copy(
            src_ref=src,
            dst_ref=dst,
            send_sem=ssem.at[sem],
            recv_sem=rsem.at[sem if rsem_at is None else rsem_at],
            device_id=to,
            device_id_type=MESH,
        )

    x_peer = dev(1 - xl, z, xh, y, c)
    w_peer = dev(1 - xl, z, 1 - xh, y, c)
    c_peer = dev(xl, z, xh, y, 1 - c)
    z_next = dev(xl, lax.rem(z + 1, 8), xh, y, c)
    z_prev = dev(xl, lax.rem(z + 7, 8), xh, y, c)

    share = y * 2 + c

    def token_rows(h):
        return pl.ds(pl.multiple_of((h * 8 + share) * TOK, TOK), TOK)

    stat_in = [
        pltpu.make_async_copy(streams[k].at[token_rows(h)], sc.at[k, h], lsem.at[k * 2 + h])
        for k in range(2)
        for h in range(2)
    ]
    stream_in_own = [pltpu.make_async_copy(streams[k], sv.at[k], lsem.at[4 + k]) for k in range(2)]
    expand_in = [pltpu.make_async_copy(expands[k], ev.at[k], lsem.at[6 + k]) for k in range(2)]
    project_in = [pltpu.make_async_copy(projects[k], pv.at[k], lsem.at[8 + k]) for k in range(2)]
    for cp in stat_in + stream_in_own[:1] + expand_in + stream_in_own[1:] + project_in:
        cp.start()

    barrier = pltpu.get_barrier_semaphore()

    def greet(d, _):
        pl.semaphore_signal(barrier, inc=1, device_id=(lax.rem(i + d, 16), j), device_id_type=MESH)
        pl.semaphore_signal(barrier, inc=1, device_id=(i, lax.rem(j + d, 16)), device_id_type=MESH)
        return 0

    lax.fori_loop(1, 16, greet, 0)
    pl.semaphore_signal(barrier, inc=1, device_id=w_peer, device_id_type=MESH)

    @pl.when(i != j)
    def _():
        pl.semaphore_signal(barrier, inc=1, device_id=(j, i), device_id_type=MESH)

    for k in range(2):
        for h in range(2):
            stat_in[k * 2 + h].wait()
            v = sc[k, h].astype(F32)
            for n, col in enumerate((v, v * v)):
                total = jnp.sum(col, axis=1, keepdims=True)
                at_row = h * 4 + k * 2 + n
                st1[at_row : at_row + 1, :] = jnp.broadcast_to(total, (TOK, TOK)).T[0:1, :]
    r1[0] = st1[...]

    @pl.when(i != j)
    def _():
        pl.semaphore_wait(barrier, 32)

    @pl.when(i == j)
    def _():
        pl.semaphore_wait(barrier, 31)

    sent, ends = [], []

    def drain():
        for cp in sent:
            cp.wait_send()
        for end in ends:
            end()

    def start(cp):
        cp.start()
        sent.append(cp)
        return cp

    def nth_chunk(n):
        return lax.rem(z + 4 + (1 - 2 * lax.rem(n, 2)) * lax.div(n + 1, 2) + 8, 8)

    half_rows = pl.ds(pl.multiple_of(c * 64, 64), 64)

    def stream_copy(k, n):
        r = nth_chunk(n)
        rows = pl.multiple_of(((1 - xl) * 8 + r) * TOK + c * 64, 64)
        return copy(
            streams[k].at[pl.ds(rows, 64)], xs.at[k, r, half_rows], S_STREAM[k] + n, w_peer
        )

    def stream_forward(k, n):
        piece = xs.at[k, nth_chunk(n), half_rows]
        return copy(piece, piece, S_STREAM[k] + 8 + n, c_peer)

    def cols(h):
        return slice(h * W, (h + 1) * W)

    exp_cp = [
        [copy(expands[k].at[:, cols(h)], xe.at[k, h], S_EXP[k] + h, x_peer) for h in range(2)]
        for k in range(2)
    ]
    prj_cp = [copy(projects[k], xp.at[k], S_PROJ[k], x_peer) for k in range(2)]
    gain_cp = [copy(gains[k], xg[k], S_GAIN[k], x_peer) for k in range(2)]
    mine = pl.ds(pl.multiple_of(j * TOK, TOK), TOK)

    def stat1(d):
        return copy(st1, r1.at[d], S_STAT1 + d, (lax.rem(i + d, 16), j))

    def stat2(d):
        return copy(st2, r2.at[share], S_STAT2 + d, (i, xh * 8 + lax.rem(share + d, 8)))

    def run(fn, lo=1, hi=16):
        def body(d, _):
            fn(d)
            return 0

        lax.fori_loop(lo, hi, body, 0)

    run(lambda d: stat1(d).start())
    ends.append(lambda: run(lambda d: stat1(d).wait_send()))
    start(gain_cp[0])
    start(gain_cp[1])
    start(exp_cp[0][0])
    run(lambda n: stream_copy(0, n).start(), 0, 8)
    start(exp_cp[0][1])
    run(lambda d: stat1(d).wait_recv())
    totals = r1[0]
    for d in range(1, 16):
        totals = totals + r1[d]
    totals = totals * (1.0 / 6144.0)
    totals = jnp.where(xl == 0, totals[0:4, :], totals[4:8, :])
    st2[...] = jnp.zeros((8, TOK), F32)
    for k in range(2):
        mean = totals[2 * k : 2 * k + 1, :]
        var = totals[2 * k + 1 : 2 * k + 2, :] - mean * mean
        st2[2 * k : 2 * k + 1, :] = mean
        st2[2 * k + 1 : 2 * k + 2, :] = lax.rsqrt(var + EPS)
    r2[share] = st2[...]
    run(lambda d: stat2(d).start(), 1, 8)
    ends.append(lambda: run(lambda d: stat2(d).wait_send(), 1, 8))
    run(lambda d: stat2(d).wait_recv(), 1, 8)

    def normalise(k, part, r):
        t = xl * 8 + r
        stats = r2[r]
        mean = spread(stats[2 * k : 2 * k + 1, :])
        rstd = spread(stats[2 * k + 1 : 2 * k + 2, :])
        if part == 0:
            v = sv[k, pl.ds(pl.multiple_of(t * TOK, TOK), TOK), :]
            gain = gains[k][...]
        else:
            v = xs[k, r]
            gain = xg[k][...]
        mean, rstd = (jnp.concatenate([q, q, q], axis=1) for q in (mean, rstd))
        nrm[k, r, part] = ((v.astype(F32) - mean) * rstd * gain.reshape(1, W)).astype(BF16)

    def pass_on(k, lo, hi):
        def one(n):
            stream_copy(k, n).wait_recv()
            stream_forward(k, n).start()

        run(one, lo, hi)

    def prepare(k, lo, hi):
        def one(n):
            stream_forward(k, n).wait_recv()
            normalise(k, 1, nth_chunk(n))

        run(one, lo, hi)

    def partial_pre(k, r, h):
        own = jnp.dot(nrm[k, r, 0], ev[k, :, cols(h)], preferred_element_type=F32)
        return own + jnp.dot(nrm[k, r, 1], xe[k, h], preferred_element_type=F32)

    def piece(ref, u):
        return ref.at[pl.ds(u * 64, 64)]

    def rs_copy(k, s, way, half, u):
        sem = S_RS[k] + 8 * s + 4 * way + 2 * half + u
        src, dst = rsb.at[k, s, way, half], rr.at[k, s, way, half]
        return copy(piece(src, u), piece(dst, u), sem, (z_next, z_prev)[way])

    def rs_step(k, s, half):
        ways = [way for way in range(2) if s > 0 or half == way]
        own = {}
        for way in ways:
            r = lax.rem(z + 4 - s + 8, 8) if way == 0 else lax.rem(z + 4 + s, 8)
            own[way] = partial_pre(k, r, half)
        for u in range(2):
            rows = slice(u * 64, (u + 1) * 64)
            for way in ways:
                acc = own[way][rows]
                if s > 1 or (s == 1 and half == way):
                    rs_copy(k, s - 1, way, half, u).wait_recv()
                    acc = acc + rr[k, s - 1, way, half, rows].astype(F32)
                rsb[k, s, way, half, rows] = acc.astype(BF16)
                rs_copy(k, s, way, half, u).start()

    def rs_sent(k):
        for u in range(2):
            for way in range(2):
                rs_copy(k, 0, way, way, u).wait_send()
                for half in range(2):
                    run(lambda s: rs_copy(k, s, way, half, u).wait_send(), 1, 4)

    def rs_finish(k):
        for half in range(2):
            acc = partial_pre(k, z, half) + shifts[k][cols(half)].reshape(1, W)
            for way in range(2):
                for u in range(2):
                    rs_copy(k, 3, way, half, u).wait_recv()
                acc = acc + rr[k, 3, way, half].astype(F32)
            act[k, z, half] = (0.5 * acc * (1.0 + lax.erf(acc * (0.5 ** 0.5)))).astype(BF16)

    def ag_copy(k, s, way, half, u):
        if way == 0:
            r, to = lax.rem(z - s + 8, 8), z_next
        else:
            r, to = lax.rem(z + s, 8), z_prev
        ref = piece(act.at[k, r, half], u)
        return copy(ref, ref, S_AG[k] + 8 * s + 4 * way + 2 * half + u, to)

    def ag_step(k, s, first=False, last=False):
        for half in range(2):
            for u in range(2):
                for way in range(2):
                    if not first:
                        ag_copy(k, s - 1, way, half, u).wait_recv()
                    if not last or half == way:
                        ag_copy(k, s, way, half, u).start()

    def ag_finish(k):
        for u in range(2):
            for way in range(2):
                ag_copy(k, 3, way, way, u).wait_recv()

    def ag_sent(k):
        for u in range(2):
            for way in range(2):
                for half in range(2):
                    run(lambda s: ag_copy(k, s, way, half, u).wait_send(), 0, 3)
                ag_copy(k, 3, way, way, u).wait_send()

    def gemm2(k, r):
        for b, weight in enumerate((pv.at[k], xp.at[k])):
            out = jnp.dot(act[k, r, 0], weight[0:W, :], preferred_element_type=F32)
            out = out + jnp.dot(act[k, r, 1], weight[W:HID, :], preferred_element_type=F32)
            yb[k, lax.rem(r, 2), b, lax.div(r, 2)] = out.astype(BF16)

    def core_copy(k, b):
        return copy(yb.at[k, 1 - c, b], cr.at[k, b], S_CORE[k] + b, c_peer)

    def core_start(k):
        for b in (1, 0):
            start(core_copy(k, b))

    def y_copy(k, d, b):
        to = dev(xl, z, xh, lax.rem(y + d, 4), c)
        return copy(ys.at[k, d - 1, b], yr.at[k, d - 1, b], S_Y[k] + 2 * d + b, to)

    def chip_sum(k, t, b):
        return yb[k, c, b, t].astype(F32) + cr[k, b, t].astype(F32)

    def y_start(k):
        for b in (1, 0):
            core_copy(k, b).wait_recv()
            for d in (2, 1, 3):
                ys[k, d - 1, b] = chip_sum(k, lax.rem(y + d, 4), b).astype(BF16)
                start(y_copy(k, d, b))

    def x_copy_a(k):
        return copy(
            xt.at[k, 1], xr.at[k, xh], S_X[k], dev(1 - xl, z, xl, y, c), S_X[k] + xh
        )

    def x_copy_a_in(k, n):
        return copy(xt.at[k, 1], xr.at[k, n], S_X[k], x_peer, S_X[k] + n)

    def x_copy_b(k):
        return copy(xt.at[k, 0], xr.at[k, 2], S_X[k] + 2, dev(xl, z, 1 - xh, y, c))

    def x_start(k):
        for b in (1, 0):
            total = chip_sum(k, y, b)
            for d in (1, 3, 2):
                y_copy(k, d, b).wait_recv()
                total = total + yr[k, d - 1, b].astype(F32)
            xt[k, b] = total.astype(BF16)
            if b == 1:
                start(x_copy_a(k))
            else:

                @pl.when(xh != xl)
                def _():
                    x_copy_b(k).start()

    def finish(k):
        def put(branch):
            resid = sv[k, mine, :].astype(F32) + offsets[k][...].reshape(1, W)
            afters[k][...] = (resid + branch).astype(BF16)

        @pl.when(xh != xl)
        def _():
            x_copy_a_in(k, 0).wait_recv()
            x_copy_a_in(k, 1).wait_recv()
            put(xr[k, 0].astype(F32) + xr[k, 1].astype(F32))
            x_copy_b(k).wait_send()

        @pl.when(xh == xl)
        def _():
            x_copy_b(k).wait_recv()
            put(xt[k, 0].astype(F32) + xr[k, 2].astype(F32))

    gain_cp[0].wait_recv()
    gain_cp[1].wait_recv()
    stream_in_own[0].wait()
    expand_in[0].wait()
    pass_on(0, 0, 3)
    run(lambda r: normalise(0, 0, r), 0, 8)
    prepare(0, 0, 3)
    exp_cp[0][0].wait_recv()
    rs_step(0, 0, 0)
    pass_on(0, 3, 8)
    run(lambda n: stream_copy(1, n).start(), 0, 8)
    rs_step(0, 1, 0)
    prepare(0, 3, 5)
    exp_cp[0][1].wait_recv()
    start(exp_cp[1][0])
    start(exp_cp[1][1])
    rs_step(0, 0, 1)
    rs_step(0, 2, 0)
    prepare(0, 5, 8)
    rs_step(0, 1, 1)
    rs_step(0, 3, 0)
    stream_in_own[1].wait()
    run(lambda r: normalise(1, 0, r), 0, 8)
    rs_step(0, 2, 1)
    pass_on(1, 0, 8)
    rs_step(0, 3, 1)
    prepare(1, 0, 8)
    for k in range(2):
        ends.append(lambda k=k: run(lambda n: stream_copy(k, n).wait_send(), 0, 8))
        ends.append(lambda k=k: run(lambda n: stream_forward(k, n).wait_send(), 0, 8))
    ends.append(lambda: rs_sent(0))

    expand_in[1].wait()
    exp_cp[1][0].wait_recv()
    rs_step(1, 0, 0)
    exp_cp[1][1].wait_recv()
    start(prj_cp[0])
    rs_step(1, 0, 1)
    rs_finish(0)
    ag_step(0, 0, True)
    for s in range(1, 4):
        rs_step(1, s, 0)
        rs_step(1, s, 1)
        ag_step(0, s, last=s == 3)
        if s == 2:
            start(prj_cp[1])
    rs_finish(1)
    ag_step(1, 0, True)
    ends.append(lambda: rs_sent(1))
    ends.append(lambda: ag_sent(0))

    def gemm2_pair(k, s):
        gemm2(k, lax.rem(z - s + 8, 8))
        gemm2(k, lax.rem(z + s, 8))

    project_in[0].wait()
    project_in[1].wait()
    prj_cp[0].wait_recv()
    gemm2(0, z)
    gemm2_pair(0, 1)
    gemm2_pair(0, 2)
    ag_finish(0)
    gemm2_pair(0, 3)
    gemm2(0, lax.rem(z + 4, 8))
    core_start(0)

    place = xh * 4 + y

    def left_copy(d):
        to = lax.rem(place + d, 8)
        return copy(a_l, al.at[share, xh], S_LEFT + d, (i, to * 2 + c))

    def left_forward(d):
        came = lax.rem(place - d + 8, 8)
        ref = al.at[lax.rem(came, 4) * 2 + c, lax.div(came, 4)]
        return copy(ref, ref, S_LEFTC + d, c_peer)

    def left_pass(d):
        left_copy(d).wait_recv()
        left_forward(d).start()

    ag_step(1, 1)
    y_start(0)
    prj_cp[1].wait_recv()
    gemm2(1, z)
    gemm2_pair(1, 1)
    ag_step(1, 2)
    gemm2_pair(1, 2)
    ag_step(1, 3, last=True)
    gemm2_pair(1, 3)
    x_start(0)
    finish(0)
    al[share, xh] = a_l[...]
    run(lambda d: left_copy(d).start(), 1, 8)
    left_forward(0).start()
    ends.append(lambda: run(lambda d: left_copy(d).wait_send(), 1, 8))
    ends.append(lambda: run(lambda d: left_forward(d).wait_send(), 0, 8))
    ag_finish(1)
    ends.append(lambda: ag_sent(1))
    gemm2(1, lax.rem(z + 4, 8))
    core_start(1)
    y_start(1)
    run(left_pass, 1, 8)
    x_start(1)
    finish(1)

    def turn(u):
        there = piece(at.at[lax.rem(j, 8), lax.div(j, 8)], u)
        return copy(piece(a_r, u), there, S_TURN + u, (j, i))

    @pl.when(i != j)
    def _():
        turn(0).start()
        turn(1).start()

    @pl.when(i == j)
    def _():
        at[z, xl] = a_r[...]

    def pair(u):
        here = piece(at.at[z, xl], u)
        return copy(here, here, S_PAIR + u, x_peer)

    def right_copy(s, way, which, u):
        if way == 0:
            r, to = lax.rem(z - s + 8, 8), z_next
        else:
            r, to = lax.rem(z + s, 8), z_prev
        ref = piece(at.at[r, xl if which == 0 else 1 - xl], u)
        return copy(ref, ref, S_RIGHT + 8 * s + 4 * way + 2 * which + u, to)

    def add(r, first=False):
        term = lax.dot_general(
            al[r].reshape(2 * TOK, W),
            at[r].reshape(2 * TOK, W),
            (((0,), (0,)), ((), ())),
            preferred_element_type=F32,
        )
        corr[...] = term if first else corr[...] + term

    def across(n, u):
        ref = piece(at.at[lax.rem(z + (5, 3, 4)[n], 8), xl], u)
        return copy(ref, ref, S_CROSS + 2 * n + u, x_peer)

    def add_pair(s):
        add(lax.rem(z - s + 8, 8))
        add(lax.rem(z + s, 8))

    for u in range(2):

        @pl.when(i != j)
        def _(u=u):
            turn(u).wait_recv()

        for way in range(2):
            start(right_copy(0, way, 0, u))
        start(pair(u))
    for u in range(2):
        pair(u).wait_recv()
        for way in range(2):
            start(right_copy(0, way, 1, u))
    for s, which in ((1, 0), (1, 1), (2, 0)):
        for u in range(2):
            for way in range(2):
                right_copy(s - 1, way, which, u).wait_recv()
                start(right_copy(s, way, which, u))
    run(lambda d: left_forward(d).wait_recv(), 0, 8)
    add(z, True)
    add_pair(1)
    for u in range(2):
        right_copy(2, 0, 0, u).wait_recv()
        start(right_copy(3, 0, 0, u))
        start(across(0, u))
        right_copy(2, 1, 0, u).wait_recv()
        start(across(1, u))
    for u in range(2):
        for way in range(2):
            right_copy(1, way, 1, u).wait_recv()
    add_pair(2)
    for u in range(2):
        right_copy(3, 0, 0, u).wait_recv()
        start(across(2, u))
    for n in range(2):
        for u in range(2):
            across(n, u).wait_recv()
    add_pair(3)
    for u in range(2):
        across(2, u).wait_recv()
    add(lax.rem(z + 4, 8))

    @pl.when(i != j)
    def _():
        turn(0).wait_send()
        turn(1).wait_send()

    drain()


def hand_out(a_l, a_r, corr, a_l_out, a_r_out, corr_out):
    a_l_out[...] = a_l[...]
    a_r_out[...] = a_r[...]
    corr_out[...] = corr[...] * (1.0 / 2048.0)


def per_device(s_l, s_r, g_l, g_r, e_l, e_r, b_l, b_r, p_l, p_r, o_l, o_r):
    vm = pl.BlockSpec(memory_space=pltpu.VMEM)
    hbm = pl.BlockSpec(memory_space=pl.ANY)
    tile = (TOK, W)
    shapes = (
        jax.ShapeDtypeStruct(tile, BF16),
        jax.ShapeDtypeStruct(tile, BF16),
        jax.ShapeDtypeStruct((W, W), F32),
    )
    results = pl.pallas_call(
        kernel,
        out_shape=shapes,
        in_specs=[hbm, hbm, vm, vm, hbm, hbm, vm, vm, hbm, hbm, vm, vm],
        out_specs=(vm, vm, vm),
        scratch_shapes=[
            pltpu.VMEM((8, TOK), F32),
            pltpu.VMEM((8, TOK), F32),
            pltpu.VMEM((16, 8, TOK), F32),
            pltpu.VMEM((8, 8, TOK), F32),
            pltpu.VMEM((2, 2, W, W), BF16),
            pltpu.VMEM((2, HID, W), BF16),
            pltpu.VMEM((W,), F32),
            pltpu.VMEM((W,), F32),
            pltpu.VMEM((2, 8) + tile, BF16),
            pltpu.VMEM((2, 8, 2) + tile, BF16),
            pltpu.VMEM((2, 4, 2, 2) + tile, BF16),
            pltpu.VMEM((2, 4, 2, 2) + tile, BF16),
            pltpu.VMEM((2, 8, 2) + tile, BF16),
            pltpu.VMEM((2, 2, 2, 4) + tile, BF16),
            pltpu.VMEM((2, 2, 4) + tile, BF16),
            pltpu.VMEM((2, 3, 2) + tile, BF16),
            pltpu.VMEM((2, 3, 2) + tile, BF16),
            pltpu.VMEM((2, 2) + tile, BF16),
            pltpu.VMEM((2, 3) + tile, BF16),
            pltpu.VMEM((8, 2) + tile, BF16),
            pltpu.VMEM((8, 2) + tile, BF16),
            pltpu.VMEM((2, 2) + tile, BF16),
            pltpu.VMEM((2, 2048, W), BF16),
            pltpu.VMEM((2, W, HID), BF16),
            pltpu.VMEM((2, HID, W), BF16),
            pltpu.SemaphoreType.DMA((N_SEMS,)),
            pltpu.SemaphoreType.DMA((N_SEMS,)),
            pltpu.SemaphoreType.DMA((10,)),
        ],
        compiler_params=pltpu.CompilerParams(
            collective_id=0, has_side_effects=True, vmem_limit_bytes=56 * 1024 * 1024
        ),
    )(s_l, s_r, g_l, g_r, e_l, e_r, b_l, b_r, p_l, p_r, o_l, o_r)
    return pl.pallas_call(
        hand_out,
        out_shape=shapes,
        in_specs=[vm] * 3,
        out_specs=(vm,) * 3,
    )(*results)


def solution(mesh):
    placed = (
        P(None, "dp"),
        P(None, "dp"),
        P("dp"),
        P("dp"),
        P("dp", "mp"),
        P("dp", "mp"),
        P("mp"),
        P("mp"),
        P("mp", "dp"),
        P("mp", "dp"),
        P("dp"),
        P("dp"),
    )
    return jax.shard_map(
        per_device,
        mesh=mesh,
        in_specs=placed,
        out_specs=(P("mp", "dp"), P("mp", "dp"), P("dp", "mp")),
        check_vma=False,
    )
```

```python
import functools

import jax
import jax.numpy as jnp
from jax import lax
from jax.experimental import pallas as pl
from jax.experimental.pallas import tpu as pltpu
from jax.sharding import PartitionSpec as P

EPS = 1e-06
F32 = jnp.float32
BF16 = jnp.bfloat16
MESH = pl.DeviceIdType.MESH

NZ, NY = 8, 4
TOK = 128
W = 384
HID = 768


class Slots:
    def __init__(self):
        self.count = 0

    def take(self, n):
        first = self.count
        self.count += n
        return first


SLOTS = Slots()
S_STAT1 = SLOTS.take(16)
S_STAT2 = SLOTS.take(16)
S_EXP = [SLOTS.take(2) for _ in range(2)]
S_PROJ = [SLOTS.take(1) for _ in range(2)]
S_GAIN = [SLOTS.take(1) for _ in range(2)]
S_STREAM = [SLOTS.take(16) for _ in range(2)]
S_RS = [SLOTS.take(32) for _ in range(2)]
S_AG = [SLOTS.take(32) for _ in range(2)]
S_CORE = [SLOTS.take(2) for _ in range(2)]
S_Y = [SLOTS.take(8) for _ in range(2)]
S_X = [SLOTS.take(3) for _ in range(2)]
S_LEFT = SLOTS.take(8)
S_LEFTC = SLOTS.take(8)
S_LEFTX = SLOTS.take(1)
S_TURN = SLOTS.take(2)
S_PAIR = SLOTS.take(2)
S_RIGHT = SLOTS.take(32)
S_CROSS = SLOTS.take(6)
N_SEMS = SLOTS.count


def spread(row, size=TOK):
    return jnp.broadcast_to(row, (size, size)).T


def kernel(
    s_l, s_r, g_l, g_r, e_l, e_r, b_l, b_r, p_l, p_r, o_l, o_r,
    a_l, a_r, corr,
    st1, st2, r1, r2, xe, xp, xg0, xg1, xs, nrm, rr, rsb, act, yb, cr, ys, yr, xt, xr, al, at,
    sc, sv, ev, pv, ssem, rsem, lsem,
):
    streams, gains, expands, shifts = (s_l, s_r), (g_l, g_r), (e_l, e_r), (b_l, b_r)
    projects, offsets, afters, xg = (p_l, p_r), (o_l, o_r), (a_l, a_r), (xg0, xg1)
    i, j = lax.axis_index("dp"), lax.axis_index("mp")
    xl, z = lax.div(i, 8), lax.rem(i, 8)
    xh, y, c = lax.div(j, 8), lax.rem(lax.div(j, 2), 4), lax.rem(j, 2)

    def dev(xl_, z_, xh_, y_, c_):
        return (xl_ * 8 + z_, xh_ * 8 + y_ * 2 + c_)

    def copy(src, dst, sem, to, rsem_at=None):
        return pltpu.make_async_remote_copy(
            src_ref=src,
            dst_ref=dst,
            send_sem=ssem.at[sem],
            recv_sem=rsem.at[sem if rsem_at is None else rsem_at],
            device_id=to,
            device_id_type=MESH,
        )

    x_peer = dev(1 - xl, z, xh, y, c)
    w_peer = dev(1 - xl, z, 1 - xh, y, c)
    c_peer = dev(xl, z, xh, y, 1 - c)
    z_next = dev(xl, lax.rem(z + 1, 8), xh, y, c)
    z_prev = dev(xl, lax.rem(z + 7, 8), xh, y, c)

    share = y * 2 + c

    def token_rows(h):
        return pl.ds(pl.multiple_of((h * 8 + share) * TOK, TOK), TOK)

    stat_in = [
        pltpu.make_async_copy(streams[k].at[token_rows(h)], sc.at[k, h], lsem.at[k * 2 + h])
        for k in range(2)
        for h in range(2)
    ]
    stream_in_own = [pltpu.make_async_copy(streams[k], sv.at[k], lsem.at[4 + k]) for k in range(2)]
    expand_in = [pltpu.make_async_copy(expands[k], ev.at[k], lsem.at[6 + k]) for k in range(2)]
    project_in = [pltpu.make_async_copy(projects[k], pv.at[k], lsem.at[8 + k]) for k in range(2)]
    for cp in stat_in + stream_in_own[:1] + expand_in + stream_in_own[1:] + project_in:
        cp.start()

    barrier = pltpu.get_barrier_semaphore()

    def greet(d, _):
        pl.semaphore_signal(barrier, inc=1, device_id=(lax.rem(i + d, 16), j), device_id_type=MESH)
        pl.semaphore_signal(barrier, inc=1, device_id=(i, lax.rem(j + d, 16)), device_id_type=MESH)
        return 0

    lax.fori_loop(1, 16, greet, 0)
    pl.semaphore_signal(barrier, inc=1, device_id=w_peer, device_id_type=MESH)

    @pl.when(i != j)
    def _():
        pl.semaphore_signal(barrier, inc=1, device_id=(j, i), device_id_type=MESH)

    for k in range(2):
        for h in range(2):
            stat_in[k * 2 + h].wait()
            v = sc[k, h].astype(F32)
            for n, col in enumerate((v, v * v)):
                total = jnp.sum(col, axis=1, keepdims=True)
                at_row = h * 4 + k * 2 + n
                st1[at_row : at_row + 1, :] = jnp.broadcast_to(total, (TOK, TOK)).T[0:1, :]
    r1[0] = st1[...]

    @pl.when(i != j)
    def _():
        pl.semaphore_wait(barrier, 32)

    @pl.when(i == j)
    def _():
        pl.semaphore_wait(barrier, 31)

    sent, ends = [], []

    def drain():
        for cp in sent:
            cp.wait_send()
        for end in ends:
            end()

    def start(cp):
        cp.start()
        sent.append(cp)
        return cp

    def nth_chunk(n):
        return lax.rem(z + 4 + (1 - 2 * lax.rem(n, 2)) * lax.div(n + 1, 2) + 8, 8)

    half_rows = pl.ds(pl.multiple_of(c * 64, 64), 64)

    def stream_copy(k, n):
        r = nth_chunk(n)
        rows = pl.multiple_of(((1 - xl) * 8 + r) * TOK + c * 64, 64)
        return copy(
            streams[k].at[pl.ds(rows, 64)], xs.at[k, r, half_rows], S_STREAM[k] + n, w_peer
        )

    def stream_forward(k, n):
        piece = xs.at[k, nth_chunk(n), half_rows]
        return copy(piece, piece, S_STREAM[k] + 8 + n, c_peer)

    def cols(h):
        return slice(h * W, (h + 1) * W)

    exp_cp = [
        [copy(expands[k].at[:, cols(h)], xe.at[k, h], S_EXP[k] + h, x_peer) for h in range(2)]
        for k in range(2)
    ]
    prj_cp = [copy(projects[k], xp.at[k], S_PROJ[k], x_peer) for k in range(2)]
    gain_cp = [copy(gains[k], xg[k], S_GAIN[k], x_peer) for k in range(2)]
    mine = pl.ds(pl.multiple_of(j * TOK, TOK), TOK)

    def stat1(d):
        return copy(st1, r1.at[d], S_STAT1 + d, (lax.rem(i + d, 16), j))

    def stat2(d):
        return copy(st2, r2.at[share], S_STAT2 + d, (i, xh * 8 + lax.rem(share + d, 8)))

    def run(fn, lo=1, hi=16):
        def body(d, _):
            fn(d)
            return 0

        lax.fori_loop(lo, hi, body, 0)

    run(lambda d: stat1(d).start())
    ends.append(lambda: run(lambda d: stat1(d).wait_send()))
    start(gain_cp[0])
    start(gain_cp[1])
    start(exp_cp[0][0])
    run(lambda n: stream_copy(0, n).start(), 0, 8)
    start(exp_cp[0][1])
    run(lambda d: stat1(d).wait_recv())
    totals = r1[0]
    for d in range(1, 16):
        totals = totals + r1[d]
    totals = totals * (1.0 / 6144.0)
    totals = jnp.where(xl == 0, totals[0:4, :], totals[4:8, :])
    st2[...] = jnp.zeros((8, TOK), F32)
    for k in range(2):
        mean = totals[2 * k : 2 * k + 1, :]
        var = totals[2 * k + 1 : 2 * k + 2, :] - mean * mean
        st2[2 * k : 2 * k + 1, :] = mean
        st2[2 * k + 1 : 2 * k + 2, :] = lax.rsqrt(var + EPS)
    r2[share] = st2[...]
    run(lambda d: stat2(d).start(), 1, 8)
    ends.append(lambda: run(lambda d: stat2(d).wait_send(), 1, 8))
    run(lambda d: stat2(d).wait_recv(), 1, 8)

    def normalise(k, part, r):
        t = xl * 8 + r
        stats = r2[r]
        mean = spread(stats[2 * k : 2 * k + 1, :])
        rstd = spread(stats[2 * k + 1 : 2 * k + 2, :])
        if part == 0:
            v = sv[k, pl.ds(pl.multiple_of(t * TOK, TOK), TOK), :]
            gain = gains[k][...]
        else:
            v = xs[k, r]
            gain = xg[k][...]
        mean, rstd = (jnp.concatenate([q, q, q], axis=1) for q in (mean, rstd))
        nrm[k, r, part] = ((v.astype(F32) - mean) * rstd * gain.reshape(1, W)).astype(BF16)

    def pass_on(k, lo, hi):
        def one(n):
            stream_copy(k, n).wait_recv()
            stream_forward(k, n).start()

        run(one, lo, hi)

    def prepare(k, lo, hi):
        def one(n):
            stream_forward(k, n).wait_recv()
            normalise(k, 1, nth_chunk(n))

        run(one, lo, hi)

    def partial_pre(k, r, h):
        own = jnp.dot(nrm[k, r, 0], ev[k, :, cols(h)], preferred_element_type=F32)
        return own + jnp.dot(nrm[k, r, 1], xe[k, h], preferred_element_type=F32)

    def piece(ref, u):
        return ref.at[pl.ds(u * 64, 64)]

    def rs_copy(k, s, way, half, u):
        sem = S_RS[k] + 8 * s + 4 * way + 2 * half + u
        src, dst = rsb.at[k, s, way, half], rr.at[k, s, way, half]
        return copy(piece(src, u), piece(dst, u), sem, (z_next, z_prev)[way])

    def rs_step(k, s, half):
        ways = [way for way in range(2) if s > 0 or half == way]
        own = {}
        for way in ways:
            r = lax.rem(z + 4 - s + 8, 8) if way == 0 else lax.rem(z + 4 + s, 8)
            own[way] = partial_pre(k, r, half)
        for u in range(2):
            rows = slice(u * 64, (u + 1) * 64)
            for way in ways:
                acc = own[way][rows]
                if s > 1 or (s == 1 and half == way):
                    rs_copy(k, s - 1, way, half, u).wait_recv()
                    acc = acc + rr[k, s - 1, way, half, rows].astype(F32)
                rsb[k, s, way, half, rows] = acc.astype(BF16)
                rs_copy(k, s, way, half, u).start()

    def rs_sent(k):
        for u in range(2):
            for way in range(2):
                rs_copy(k, 0, way, way, u).wait_send()
                for half in range(2):
                    run(lambda s: rs_copy(k, s, way, half, u).wait_send(), 1, 4)

    def rs_finish(k):
        for half in range(2):
            acc = partial_pre(k, z, half) + shifts[k][cols(half)].reshape(1, W)
            for way in range(2):
                for u in range(2):
                    rs_copy(k, 3, way, half, u).wait_recv()
                acc = acc + rr[k, 3, way, half].astype(F32)
            act[k, z, half] = (0.5 * acc * (1.0 + lax.erf(acc * (0.5 ** 0.5)))).astype(BF16)

    def ag_copy(k, s, way, half, u):
        if way == 0:
            r, to = lax.rem(z - s + 8, 8), z_next
        else:
            r, to = lax.rem(z + s, 8), z_prev
        ref = piece(act.at[k, r, half], u)
        return copy(ref, ref, S_AG[k] + 8 * s + 4 * way + 2 * half + u, to)

    def ag_step(k, s, first=False, last=False):
        for half in range(2):
            for u in range(2):
                for way in range(2):
                    if not first:
                        ag_copy(k, s - 1, way, half, u).wait_recv()
                    if not last or half == way:
                        ag_copy(k, s, way, half, u).start()

    def ag_finish(k):
        for u in range(2):
            for way in range(2):
                ag_copy(k, 3, way, way, u).wait_recv()

    def ag_sent(k):
        for u in range(2):
            for way in range(2):
                for half in range(2):
                    run(lambda s: ag_copy(k, s, way, half, u).wait_send(), 0, 3)
                ag_copy(k, 3, way, way, u).wait_send()

    def gemm2(k, r):
        for b, weight in enumerate((pv.at[k], xp.at[k])):
            out = jnp.dot(act[k, r, 0], weight[0:W, :], preferred_element_type=F32)
            out = out + jnp.dot(act[k, r, 1], weight[W:HID, :], preferred_element_type=F32)
            yb[k, lax.rem(r, 2), b, lax.div(r, 2)] = out.astype(BF16)

    def core_copy(k, b):
        return copy(yb.at[k, 1 - c, b], cr.at[k, b], S_CORE[k] + b, c_peer)

    def core_start(k):
        for b in (1, 0):
            start(core_copy(k, b))

    def y_copy(k, d, b):
        to = dev(xl, z, xh, lax.rem(y + d, 4), c)
        return copy(ys.at[k, d - 1, b], yr.at[k, d - 1, b], S_Y[k] + 2 * d + b, to)

    def chip_sum(k, t, b):
        return yb[k, c, b, t].astype(F32) + cr[k, b, t].astype(F32)

    def y_start(k):
        for b in (1, 0):
            core_copy(k, b).wait_recv()
            for d in (2, 1, 3):
                ys[k, d - 1, b] = chip_sum(k, lax.rem(y + d, 4), b).astype(BF16)
                start(y_copy(k, d, b))

    def x_copy_a(k):
        return copy(
            xt.at[k, 1], xr.at[k, xh], S_X[k], dev(1 - xl, z, xl, y, c), S_X[k] + xh
        )

    def x_copy_a_in(k, n):
        return copy(xt.at[k, 1], xr.at[k, n], S_X[k], x_peer, S_X[k] + n)

    def x_copy_b(k):
        return copy(xt.at[k, 0], xr.at[k, 2], S_X[k] + 2, dev(xl, z, 1 - xh, y, c))

    def x_start(k):
        for b in (1, 0):
            total = chip_sum(k, y, b)
            for d in (1, 3, 2):
                y_copy(k, d, b).wait_recv()
                total = total + yr[k, d - 1, b].astype(F32)
            xt[k, b] = total.astype(BF16)
            if b == 1:
                start(x_copy_a(k))
            else:

                @pl.when(xh != xl)
                def _():
                    x_copy_b(k).start()

    def finish(k):
        def put(branch):
            resid = sv[k, mine, :].astype(F32) + offsets[k][...].reshape(1, W)
            afters[k][...] = (resid + branch).astype(BF16)

        @pl.when(xh != xl)
        def _():
            x_copy_a_in(k, 0).wait_recv()
            x_copy_a_in(k, 1).wait_recv()
            put(xr[k, 0].astype(F32) + xr[k, 1].astype(F32))
            x_copy_b(k).wait_send()

        @pl.when(xh == xl)
        def _():
            x_copy_b(k).wait_recv()
            put(xt[k, 0].astype(F32) + xr[k, 2].astype(F32))

    gain_cp[0].wait_recv()
    gain_cp[1].wait_recv()
    stream_in_own[0].wait()
    expand_in[0].wait()
    pass_on(0, 0, 3)
    run(lambda r: normalise(0, 0, r), 0, 8)
    prepare(0, 0, 3)
    exp_cp[0][0].wait_recv()
    rs_step(0, 0, 0)
    pass_on(0, 3, 8)
    run(lambda n: stream_copy(1, n).start(), 0, 8)
    rs_step(0, 1, 0)
    prepare(0, 3, 5)
    exp_cp[0][1].wait_recv()
    start(exp_cp[1][0])
    start(exp_cp[1][1])
    rs_step(0, 0, 1)
    rs_step(0, 2, 0)
    prepare(0, 5, 8)
    rs_step(0, 1, 1)
    rs_step(0, 3, 0)
    stream_in_own[1].wait()
    run(lambda r: normalise(1, 0, r), 0, 8)
    rs_step(0, 2, 1)
    pass_on(1, 0, 8)
    rs_step(0, 3, 1)
    prepare(1, 0, 8)
    for k in range(2):
        ends.append(lambda k=k: run(lambda n: stream_copy(k, n).wait_send(), 0, 8))
        ends.append(lambda k=k: run(lambda n: stream_forward(k, n).wait_send(), 0, 8))
    ends.append(lambda: rs_sent(0))

    expand_in[1].wait()
    exp_cp[1][0].wait_recv()
    rs_step(1, 0, 0)
    exp_cp[1][1].wait_recv()
    start(prj_cp[0])
    rs_step(1, 0, 1)
    rs_finish(0)
    ag_step(0, 0, True)
    ag_step(0, 1)
    ag_step(0, 2)
    rs_step(1, 1, 0)
    rs_step(1, 1, 1)
    ag_step(0, 3, last=True)
    rs_step(1, 2, 0)
    rs_step(1, 2, 1)

    def gemm2_pair(k, s):
        gemm2(k, lax.rem(z - s + 8, 8))
        gemm2(k, lax.rem(z + s, 8))

    project_in[0].wait()
    project_in[1].wait()
    prj_cp[0].wait_recv()
    start(prj_cp[1])
    gemm2(0, z)
    gemm2_pair(0, 1)
    gemm2_pair(0, 2)
    rs_step(1, 3, 0)
    rs_step(1, 3, 1)
    ag_finish(0)
    gemm2_pair(0, 3)
    gemm2(0, lax.rem(z + 4, 8))
    core_start(0)
    ends.append(lambda: rs_sent(1))
    ends.append(lambda: ag_sent(0))
    rs_finish(1)

    def tile_of(far, back):
        row = lax.rem(y - back + 4, 4)
        return al.at[row * 2 + c, xh + far * (1 - 2 * xh)]

    def left_y(far, d):
        ref = tile_of(far, 0)
        return copy(ref, ref, S_LEFT + 4 * far + d, dev(xl, z, xh, lax.rem(y + d, 4), c))

    def left_x():
        ref = tile_of(0, 0)
        return copy(ref, ref, S_LEFTX, dev(xl, z, 1 - xh, y, c))

    def left_forward(n):
        ref = tile_of(lax.div(n, 4), lax.rem(n, 4))
        return copy(ref, ref, S_LEFTC + n, c_peer)

    def left_pass(far, d):
        left_y(far, d).wait_recv()
        left_forward(4 * far + d).start()

    ag_step(1, 0, True)
    y_start(0)
    ag_step(1, 1)
    prj_cp[1].wait_recv()
    gemm2(1, z)
    gemm2_pair(1, 1)
    ag_step(1, 2)
    gemm2_pair(1, 2)
    x_start(0)
    ag_step(1, 3, last=True)
    gemm2_pair(1, 3)
    finish(0)
    al[share, xh] = a_l[...]
    start(left_x())
    for d in (2, 1, 3):
        start(left_y(0, d))
    left_forward(0).start()
    ends.append(lambda: run(lambda n: left_forward(n).wait_send(), 0, 8))
    ag_finish(1)
    ends.append(lambda: ag_sent(1))
    gemm2(1, lax.rem(z + 4, 8))
    core_start(1)
    y_start(1)
    left_x().wait_recv()
    for d in (2, 1, 3):
        start(left_y(1, d))
    left_forward(4).start()
    run(lambda d: left_pass(0, d), 1, 4)
    x_start(1)
    finish(1)

    def turn(u):
        there = piece(at.at[lax.rem(j, 8), lax.div(j, 8)], u)
        return copy(piece(a_r, u), there, S_TURN + u, (j, i))

    @pl.when(i != j)
    def _():
        turn(0).start()
        turn(1).start()

    @pl.when(i == j)
    def _():
        at[z, xl] = a_r[...]

    def pair(u):
        here = piece(at.at[z, xl], u)
        return copy(here, here, S_PAIR + u, x_peer)

    def right_copy(s, way, which, u):
        if way == 0:
            r, to = lax.rem(z - s + 8, 8), z_next
        else:
            r, to = lax.rem(z + s, 8), z_prev
        ref = piece(at.at[r, xl if which == 0 else 1 - xl], u)
        return copy(ref, ref, S_RIGHT + 8 * s + 4 * way + 2 * which + u, to)

    def add(r, first=False):
        term = lax.dot_general(
            al[r].reshape(2 * TOK, W),
            at[r].reshape(2 * TOK, W),
            (((0,), (0,)), ((), ())),
            preferred_element_type=F32,
        )
        corr[...] = term if first else corr[...] + term

    def across(n, u):
        ref = piece(at.at[lax.rem(z + (5, 3, 4)[n], 8), xl], u)
        return copy(ref, ref, S_CROSS + 2 * n + u, x_peer)

    def add_pair(s):
        add(lax.rem(z - s + 8, 8))
        add(lax.rem(z + s, 8))

    for u in range(2):

        @pl.when(i != j)
        def _(u=u):
            turn(u).wait_recv()

        for way in range(2):
            start(right_copy(0, way, 0, u))
        start(pair(u))
    for u in range(2):
        pair(u).wait_recv()
        for way in range(2):
            start(right_copy(0, way, 1, u))
    for s, which in ((1, 0), (1, 1), (2, 0)):
        for u in range(2):
            for way in range(2):
                right_copy(s - 1, way, which, u).wait_recv()
                start(right_copy(s, way, which, u))
    run(lambda d: left_pass(1, d), 1, 4)
    run(lambda n: left_forward(n).wait_recv(), 0, 8)
    add(z, True)
    add_pair(1)
    for u in range(2):
        right_copy(2, 0, 0, u).wait_recv()
        start(right_copy(3, 0, 0, u))
        start(across(0, u))
        right_copy(2, 1, 0, u).wait_recv()
        start(across(1, u))
    for u in range(2):
        for way in range(2):
            right_copy(1, way, 1, u).wait_recv()
    add_pair(2)
    for u in range(2):
        right_copy(3, 0, 0, u).wait_recv()
        start(across(2, u))
    for n in range(2):
        for u in range(2):
            across(n, u).wait_recv()
    add_pair(3)
    for u in range(2):
        across(2, u).wait_recv()
    add(lax.rem(z + 4, 8))

    @pl.when(i != j)
    def _():
        turn(0).wait_send()
        turn(1).wait_send()

    drain()


def hand_out(a_l, a_r, corr, a_l_out, a_r_out, corr_out):
    a_l_out[...] = a_l[...]
    a_r_out[...] = a_r[...]
    corr_out[...] = corr[...] * (1.0 / 2048.0)


def per_device(s_l, s_r, g_l, g_r, e_l, e_r, b_l, b_r, p_l, p_r, o_l, o_r):
    vm = pl.BlockSpec(memory_space=pltpu.VMEM)
    hbm = pl.BlockSpec(memory_space=pl.ANY)
    tile = (TOK, W)
    shapes = (
        jax.ShapeDtypeStruct(tile, BF16),
        jax.ShapeDtypeStruct(tile, BF16),
        jax.ShapeDtypeStruct((W, W), F32),
    )
    results = pl.pallas_call(
        kernel,
        out_shape=shapes,
        in_specs=[hbm, hbm, vm, vm, hbm, hbm, vm, vm, hbm, hbm, vm, vm],
        out_specs=(vm, vm, vm),
        scratch_shapes=[
            pltpu.VMEM((8, TOK), F32),
            pltpu.VMEM((8, TOK), F32),
            pltpu.VMEM((16, 8, TOK), F32),
            pltpu.VMEM((8, 8, TOK), F32),
            pltpu.VMEM((2, 2, W, W), BF16),
            pltpu.VMEM((2, HID, W), BF16),
            pltpu.VMEM((W,), F32),
            pltpu.VMEM((W,), F32),
            pltpu.VMEM((2, 8) + tile, BF16),
            pltpu.VMEM((2, 8, 2) + tile, BF16),
            pltpu.VMEM((2, 4, 2, 2) + tile, BF16),
            pltpu.VMEM((2, 4, 2, 2) + tile, BF16),
            pltpu.VMEM((2, 8, 2) + tile, BF16),
            pltpu.VMEM((2, 2, 2, 4) + tile, BF16),
            pltpu.VMEM((2, 2, 4) + tile, BF16),
            pltpu.VMEM((2, 3, 2) + tile, BF16),
            pltpu.VMEM((2, 3, 2) + tile, BF16),
            pltpu.VMEM((2, 2) + tile, BF16),
            pltpu.VMEM((2, 3) + tile, BF16),
            pltpu.VMEM((8, 2) + tile, BF16),
            pltpu.VMEM((8, 2) + tile, BF16),
            pltpu.VMEM((2, 2) + tile, BF16),
            pltpu.VMEM((2, 2048, W), BF16),
            pltpu.VMEM((2, W, HID), BF16),
            pltpu.VMEM((2, HID, W), BF16),
            pltpu.SemaphoreType.DMA((N_SEMS,)),
            pltpu.SemaphoreType.DMA((N_SEMS,)),
            pltpu.SemaphoreType.DMA((10,)),
        ],
        compiler_params=pltpu.CompilerParams(
            collective_id=0, has_side_effects=True, vmem_limit_bytes=56 * 1024 * 1024
        ),
    )(s_l, s_r, g_l, g_r, e_l, e_r, b_l, b_r, p_l, p_r, o_l, o_r)
    return pl.pallas_call(
        hand_out,
        out_shape=shapes,
        in_specs=[vm] * 3,
        out_specs=(vm,) * 3,
    )(*results)


def solution(mesh):
    placed = (
        P(None, "dp"),
        P(None, "dp"),
        P("dp"),
        P("dp"),
        P("dp", "mp"),
        P("dp", "mp"),
        P("mp"),
        P("mp"),
        P("mp", "dp"),
        P("mp", "dp"),
        P("dp"),
        P("dp"),
    )
    return jax.shard_map(
        per_device,
        mesh=mesh,
        in_specs=placed,
        out_specs=(P("mp", "dp"), P("mp", "dp"), P("dp", "mp")),
        check_vma=False,
    )
```

```python
import functools

import jax
import jax.numpy as jnp
from jax import lax
from jax.experimental import pallas as pl
from jax.experimental.pallas import tpu as pltpu
from jax.sharding import PartitionSpec as P

EPS = 1e-06
F32 = jnp.float32
BF16 = jnp.bfloat16
MESH = pl.DeviceIdType.MESH

NZ, NY = 8, 4
TOK = 128
W = 384
HID = 768


class Slots:
    def __init__(self):
        self.count = 0

    def take(self, n):
        first = self.count
        self.count += n
        return first


SLOTS = Slots()
S_STAT1 = SLOTS.take(16)
S_STAT2 = SLOTS.take(16)
S_EXP = [SLOTS.take(2) for _ in range(2)]
S_PROJ = [SLOTS.take(1) for _ in range(2)]
S_GAIN = [SLOTS.take(1) for _ in range(2)]
S_STREAM = [SLOTS.take(16) for _ in range(2)]
S_RS = [SLOTS.take(32) for _ in range(2)]
S_AG = [SLOTS.take(32) for _ in range(2)]
S_CORE = [SLOTS.take(2) for _ in range(2)]
S_Y = [SLOTS.take(8) for _ in range(2)]
S_X = [SLOTS.take(3) for _ in range(2)]
S_LEFT = SLOTS.take(8)
S_LEFTC = SLOTS.take(8)
S_LEFTX = SLOTS.take(1)
S_TURN = SLOTS.take(2)
S_PAIR = SLOTS.take(2)
S_RIGHT = SLOTS.take(32)
S_CROSS = SLOTS.take(6)
N_SEMS = SLOTS.count


def spread(row, size=TOK):
    return jnp.broadcast_to(row, (size, size)).T


def kernel(
    s_l, s_r, g_l, g_r, e_l, e_r, b_l, b_r, p_l, p_r, o_l, o_r,
    a_l, a_r, corr,
    st1, st2, r1, r2, xe, xp, xg0, xg1, xs, nrm, rr, rsb, act, yb, cr, ys, yr, xt, xr, al, at,
    sc, sv, ev, pv, ssem, rsem, lsem,
):
    streams, gains, expands, shifts = (s_l, s_r), (g_l, g_r), (e_l, e_r), (b_l, b_r)
    projects, offsets, afters, xg = (p_l, p_r), (o_l, o_r), (a_l, a_r), (xg0, xg1)
    i, j = lax.axis_index("dp"), lax.axis_index("mp")
    xl, z = lax.div(i, 8), lax.rem(i, 8)
    xh, y, c = lax.div(j, 8), lax.rem(lax.div(j, 2), 4), lax.rem(j, 2)

    def dev(xl_, z_, xh_, y_, c_):
        return (xl_ * 8 + z_, xh_ * 8 + y_ * 2 + c_)

    def copy(src, dst, sem, to, rsem_at=None):
        return pltpu.make_async_remote_copy(
            src_ref=src,
            dst_ref=dst,
            send_sem=ssem.at[sem],
            recv_sem=rsem.at[sem if rsem_at is None else rsem_at],
            device_id=to,
            device_id_type=MESH,
        )

    x_peer = dev(1 - xl, z, xh, y, c)
    w_peer = dev(1 - xl, z, 1 - xh, y, c)
    c_peer = dev(xl, z, xh, y, 1 - c)
    z_next = dev(xl, lax.rem(z + 1, 8), xh, y, c)
    z_prev = dev(xl, lax.rem(z + 7, 8), xh, y, c)

    share = y * 2 + c

    def token_rows(h):
        return pl.ds(pl.multiple_of((h * 8 + share) * TOK, TOK), TOK)

    stat_in = [
        pltpu.make_async_copy(streams[k].at[token_rows(h)], sc.at[k, h], lsem.at[k * 2 + h])
        for k in range(2)
        for h in range(2)
    ]
    stream_in_own = [pltpu.make_async_copy(streams[k], sv.at[k], lsem.at[4 + k]) for k in range(2)]
    expand_in = [pltpu.make_async_copy(expands[k], ev.at[k], lsem.at[6 + k]) for k in range(2)]
    project_in = [pltpu.make_async_copy(projects[k], pv.at[k], lsem.at[8 + k]) for k in range(2)]
    for cp in stat_in + stream_in_own[:1] + expand_in + stream_in_own[1:] + project_in:
        cp.start()

    barrier = pltpu.get_barrier_semaphore()

    def greet(d, _):
        pl.semaphore_signal(barrier, inc=1, device_id=(lax.rem(i + d, 16), j), device_id_type=MESH)
        pl.semaphore_signal(barrier, inc=1, device_id=(i, lax.rem(j + d, 16)), device_id_type=MESH)
        return 0

    lax.fori_loop(1, 16, greet, 0)
    pl.semaphore_signal(barrier, inc=1, device_id=w_peer, device_id_type=MESH)

    @pl.when(i != j)
    def _():
        pl.semaphore_signal(barrier, inc=1, device_id=(j, i), device_id_type=MESH)

    for k in range(2):
        for h in range(2):
            stat_in[k * 2 + h].wait()
            v = sc[k, h].astype(F32)
            for n, col in enumerate((v, v * v)):
                total = jnp.sum(col, axis=1, keepdims=True)
                at_row = h * 4 + k * 2 + n
                st1[at_row : at_row + 1, :] = jnp.broadcast_to(total, (TOK, TOK)).T[0:1, :]
    r1[0] = st1[...]

    @pl.when(i != j)
    def _():
        pl.semaphore_wait(barrier, 32)

    @pl.when(i == j)
    def _():
        pl.semaphore_wait(barrier, 31)

    sent, ends = [], []

    def drain():
        for cp in sent:
            cp.wait_send()
        for end in ends:
            end()

    def start(cp):
        cp.start()
        sent.append(cp)
        return cp

    def nth_chunk(n):
        return lax.rem(z + 4 + (1 - 2 * lax.rem(n, 2)) * lax.div(n + 1, 2) + 8, 8)

    half_rows = pl.ds(pl.multiple_of(c * 64, 64), 64)

    def stream_copy(k, n):
        r = nth_chunk(n)
        rows = pl.multiple_of(((1 - xl) * 8 + r) * TOK + c * 64, 64)
        return copy(
            streams[k].at[pl.ds(rows, 64)], xs.at[k, r, half_rows], S_STREAM[k] + n, w_peer
        )

    def stream_forward(k, n):
        piece = xs.at[k, nth_chunk(n), half_rows]
        return copy(piece, piece, S_STREAM[k] + 8 + n, c_peer)

    def cols(h):
        return slice(h * W, (h + 1) * W)

    exp_cp = [
        [copy(expands[k].at[:, cols(h)], xe.at[k, h], S_EXP[k] + h, x_peer) for h in range(2)]
        for k in range(2)
    ]
    prj_cp = [copy(projects[k], xp.at[k], S_PROJ[k], x_peer) for k in range(2)]
    gain_cp = [copy(gains[k], xg[k], S_GAIN[k], x_peer) for k in range(2)]
    mine = pl.ds(pl.multiple_of(j * TOK, TOK), TOK)

    def stat1(d):
        return copy(st1, r1.at[d], S_STAT1 + d, (lax.rem(i + d, 16), j))

    def stat2(d):
        return copy(st2, r2.at[share], S_STAT2 + d, (i, xh * 8 + lax.rem(share + d, 8)))

    def run(fn, lo=1, hi=16):
        def body(d, _):
            fn(d)
            return 0

        lax.fori_loop(lo, hi, body, 0)

    run(lambda d: stat1(d).start())
    ends.append(lambda: run(lambda d: stat1(d).wait_send()))
    start(gain_cp[0])
    start(gain_cp[1])
    start(exp_cp[0][0])
    run(lambda n: stream_copy(0, n).start(), 0, 8)
    start(exp_cp[0][1])
    run(lambda d: stat1(d).wait_recv())
    totals = r1[0]
    for d in range(1, 16):
        totals = totals + r1[d]
    totals = totals * (1.0 / 6144.0)
    totals = jnp.where(xl == 0, totals[0:4, :], totals[4:8, :])
    st2[...] = jnp.zeros((8, TOK), F32)
    for k in range(2):
        mean = totals[2 * k : 2 * k + 1, :]
        var = totals[2 * k + 1 : 2 * k + 2, :] - mean * mean
        st2[2 * k : 2 * k + 1, :] = mean
        st2[2 * k + 1 : 2 * k + 2, :] = lax.rsqrt(var + EPS)
    r2[share] = st2[...]
    run(lambda d: stat2(d).start(), 1, 8)
    ends.append(lambda: run(lambda d: stat2(d).wait_send(), 1, 8))
    run(lambda d: stat2(d).wait_recv(), 1, 8)

    def normalise(k, part, r):
        t = xl * 8 + r
        stats = r2[r]
        mean = spread(stats[2 * k : 2 * k + 1, :])
        rstd = spread(stats[2 * k + 1 : 2 * k + 2, :])
        if part == 0:
            v = sv[k, pl.ds(pl.multiple_of(t * TOK, TOK), TOK), :]
            gain = gains[k][...]
        else:
            v = xs[k, r]
            gain = xg[k][...]
        mean, rstd = (jnp.concatenate([q, q, q], axis=1) for q in (mean, rstd))
        nrm[k, r, part] = ((v.astype(F32) - mean) * rstd * gain.reshape(1, W)).astype(BF16)

    def pass_on(k, lo, hi):
        def one(n):
            stream_copy(k, n).wait_recv()
            stream_forward(k, n).start()

        run(one, lo, hi)

    def prepare(k, lo, hi):
        def one(n):
            stream_forward(k, n).wait_recv()
            normalise(k, 1, nth_chunk(n))

        run(one, lo, hi)

    def partial_pre(k, r, h):
        own = jnp.dot(nrm[k, r, 0], ev[k, :, cols(h)], preferred_element_type=F32)
        return own + jnp.dot(nrm[k, r, 1], xe[k, h], preferred_element_type=F32)

    def piece(ref, u):
        return ref.at[pl.ds(u * 64, 64)]

    def rs_copy(k, s, way, half, u):
        sem = S_RS[k] + 8 * s + 4 * way + 2 * half + u
        src, dst = rsb.at[k, s, way, half], rr.at[k, s, way, half]
        return copy(piece(src, u), piece(dst, u), sem, (z_next, z_prev)[way])

    def rs_step(k, s, half):
        ways = [way for way in range(2) if s > 0 or half == way]
        own = {}
        for way in ways:
            r = lax.rem(z + 4 - s + 8, 8) if way == 0 else lax.rem(z + 4 + s, 8)
            own[way] = partial_pre(k, r, half)
        for u in range(2):
            rows = slice(u * 64, (u + 1) * 64)
            for way in ways:
                acc = own[way][rows]
                if s > 1 or (s == 1 and half == way):
                    rs_copy(k, s - 1, way, half, u).wait_recv()
                    acc = acc + rr[k, s - 1, way, half, rows].astype(F32)
                rsb[k, s, way, half, rows] = acc.astype(BF16)
                rs_copy(k, s, way, half, u).start()

    def rs_sent(k):
        for u in range(2):
            for way in range(2):
                rs_copy(k, 0, way, way, u).wait_send()
                for half in range(2):
                    run(lambda s: rs_copy(k, s, way, half, u).wait_send(), 1, 4)

    def rs_finish(k):
        for half in range(2):
            acc = partial_pre(k, z, half) + shifts[k][cols(half)].reshape(1, W)
            for way in range(2):
                for u in range(2):
                    rs_copy(k, 3, way, half, u).wait_recv()
                acc = acc + rr[k, 3, way, half].astype(F32)
            act[k, z, half] = (0.5 * acc * (1.0 + lax.erf(acc * (0.5 ** 0.5)))).astype(BF16)

    def ag_copy(k, s, way, half, u):
        if way == 0:
            r, to = lax.rem(z - s + 8, 8), z_next
        else:
            r, to = lax.rem(z + s, 8), z_prev
        ref = piece(act.at[k, r, half], u)
        return copy(ref, ref, S_AG[k] + 8 * s + 4 * way + 2 * half + u, to)

    def ag_step(k, s, first=False, last=False):
        for half in range(2):
            for u in range(2):
                for way in range(2):
                    if not first:
                        ag_copy(k, s - 1, way, half, u).wait_recv()
                    if not last or half == way:
                        ag_copy(k, s, way, half, u).start()

    def ag_finish(k):
        for u in range(2):
            for way in range(2):
                ag_copy(k, 3, way, way, u).wait_recv()

    def ag_sent(k):
        for u in range(2):
            for way in range(2):
                for half in range(2):
                    run(lambda s: ag_copy(k, s, way, half, u).wait_send(), 0, 3)
                ag_copy(k, 3, way, way, u).wait_send()

    def gemm2(k, r):
        for b, weight in enumerate((pv.at[k], xp.at[k])):
            out = jnp.dot(act[k, r, 0], weight[0:W, :], preferred_element_type=F32)
            out = out + jnp.dot(act[k, r, 1], weight[W:HID, :], preferred_element_type=F32)
            yb[k, lax.rem(r, 2), b, lax.div(r, 2)] = out.astype(BF16)

    def core_copy(k, b):
        return copy(yb.at[k, 1 - c, b], cr.at[k, b], S_CORE[k] + b, c_peer)

    def core_start(k):
        for b in (1, 0):
            start(core_copy(k, b))

    def y_copy(k, d, b):
        to = dev(xl, z, xh, lax.rem(y + d, 4), c)
        return copy(ys.at[k, d - 1, b], yr.at[k, d - 1, b], S_Y[k] + 2 * d + b, to)

    def chip_sum(k, t, b):
        return yb[k, c, b, t].astype(F32) + cr[k, b, t].astype(F32)

    def y_start(k):
        for b in (1, 0):
            core_copy(k, b).wait_recv()
            for d in (2, 1, 3):
                ys[k, d - 1, b] = chip_sum(k, lax.rem(y + d, 4), b).astype(BF16)
                start(y_copy(k, d, b))

    def x_copy_a(k):
        return copy(
            xt.at[k, 1], xr.at[k, xh], S_X[k], dev(1 - xl, z, xl, y, c), S_X[k] + xh
        )

    def x_copy_a_in(k, n):
        return copy(xt.at[k, 1], xr.at[k, n], S_X[k], x_peer, S_X[k] + n)

    def x_copy_b(k):
        return copy(xt.at[k, 0], xr.at[k, 2], S_X[k] + 2, dev(xl, z, 1 - xh, y, c))

    def x_start(k):
        for b in (1, 0):
            total = chip_sum(k, y, b)
            for d in (1, 3, 2):
                y_copy(k, d, b).wait_recv()
                total = total + yr[k, d - 1, b].astype(F32)
            xt[k, b] = total.astype(BF16)
            if b == 1:
                start(x_copy_a(k))
            else:

                @pl.when(xh != xl)
                def _():
                    x_copy_b(k).start()

    def finish(k):
        def put(branch):
            resid = sv[k, mine, :].astype(F32) + offsets[k][...].reshape(1, W)
            afters[k][...] = (resid + branch).astype(BF16)

        @pl.when(xh != xl)
        def _():
            x_copy_a_in(k, 0).wait_recv()
            x_copy_a_in(k, 1).wait_recv()
            put(xr[k, 0].astype(F32) + xr[k, 1].astype(F32))
            x_copy_b(k).wait_send()

        @pl.when(xh == xl)
        def _():
            x_copy_b(k).wait_recv()
            put(xt[k, 0].astype(F32) + xr[k, 2].astype(F32))

    gain_cp[0].wait_recv()
    gain_cp[1].wait_recv()
    stream_in_own[0].wait()
    expand_in[0].wait()
    pass_on(0, 0, 3)
    run(lambda r: normalise(0, 0, r), 0, 8)
    prepare(0, 0, 3)
    exp_cp[0][0].wait_recv()
    rs_step(0, 0, 0)
    pass_on(0, 3, 8)
    run(lambda n: stream_copy(1, n).start(), 0, 8)
    rs_step(0, 1, 0)
    prepare(0, 3, 5)
    exp_cp[0][1].wait_recv()
    start(exp_cp[1][0])
    start(exp_cp[1][1])
    rs_step(0, 0, 1)
    rs_step(0, 2, 0)
    prepare(0, 5, 8)
    rs_step(0, 1, 1)
    rs_step(0, 3, 0)
    stream_in_own[1].wait()
    run(lambda r: normalise(1, 0, r), 0, 8)
    rs_step(0, 2, 1)
    pass_on(1, 0, 8)
    rs_step(0, 3, 1)
    prepare(1, 0, 8)
    for k in range(2):
        ends.append(lambda k=k: run(lambda n: stream_copy(k, n).wait_send(), 0, 8))
        ends.append(lambda k=k: run(lambda n: stream_forward(k, n).wait_send(), 0, 8))
    ends.append(lambda: rs_sent(0))

    expand_in[1].wait()
    exp_cp[1][0].wait_recv()
    rs_step(1, 0, 0)
    exp_cp[1][1].wait_recv()
    start(prj_cp[0])
    rs_step(1, 0, 1)
    rs_finish(0)
    ag_step(0, 0, True)
    for s in range(1, 4):
        rs_step(1, s, 0)
        rs_step(1, s, 1)
        ag_step(0, s, last=s == 3)
        if s == 2:
            start(prj_cp[1])
    rs_finish(1)
    ag_step(1, 0, True)
    ends.append(lambda: rs_sent(1))
    ends.append(lambda: ag_sent(0))

    def gemm2_pair(k, s):
        gemm2(k, lax.rem(z - s + 8, 8))
        gemm2(k, lax.rem(z + s, 8))

    project_in[0].wait()
    project_in[1].wait()
    prj_cp[0].wait_recv()
    gemm2(0, z)
    gemm2_pair(0, 1)
    gemm2_pair(0, 2)
    ag_finish(0)
    gemm2_pair(0, 3)
    gemm2(0, lax.rem(z + 4, 8))
    core_start(0)

    def tile_of(far, back):
        row = lax.rem(y - back + 4, 4)
        return al.at[row * 2 + c, xh + far * (1 - 2 * xh)]

    def left_y(far, d):
        ref = tile_of(far, 0)
        return copy(ref, ref, S_LEFT + 4 * far + d, dev(xl, z, xh, lax.rem(y + d, 4), c))

    def left_x():
        ref = tile_of(0, 0)
        return copy(ref, ref, S_LEFTX, dev(xl, z, 1 - xh, y, c))

    def left_forward(n):
        ref = tile_of(lax.div(n, 4), lax.rem(n, 4))
        return copy(ref, ref, S_LEFTC + n, c_peer)

    def left_pass(far, d):
        left_y(far, d).wait_recv()
        left_forward(4 * far + d).start()

    ag_step(1, 1)
    y_start(0)
    prj_cp[1].wait_recv()
    gemm2(1, z)
    gemm2_pair(1, 1)
    ag_step(1, 2)
    gemm2_pair(1, 2)
    ag_step(1, 3, last=True)
    gemm2_pair(1, 3)
    x_start(0)
    ag_finish(1)
    ends.append(lambda: ag_sent(1))
    gemm2(1, lax.rem(z + 4, 8))
    core_start(1)
    finish(0)
    y_start(1)
    al[share, xh] = a_l[...]
    start(left_x())
    for d in (2, 1, 3):
        start(left_y(0, d))
    left_forward(0).start()
    ends.append(lambda: run(lambda n: left_forward(n).wait_send(), 0, 8))
    left_x().wait_recv()
    for d in (2, 1, 3):
        start(left_y(1, d))
    left_forward(4).start()
    x_start(1)
    run(lambda d: left_pass(0, d), 1, 4)
    finish(1)

    def turn(u):
        there = piece(at.at[lax.rem(j, 8), lax.div(j, 8)], u)
        return copy(piece(a_r, u), there, S_TURN + u, (j, i))

    @pl.when(i != j)
    def _():
        turn(0).start()
        turn(1).start()

    @pl.when(i == j)
    def _():
        at[z, xl] = a_r[...]

    def pair(u):
        here = piece(at.at[z, xl], u)
        return copy(here, here, S_PAIR + u, x_peer)

    def right_copy(s, way, which, u):
        if way == 0:
            r, to = lax.rem(z - s + 8, 8), z_next
        else:
            r, to = lax.rem(z + s, 8), z_prev
        ref = piece(at.at[r, xl if which == 0 else 1 - xl], u)
        return copy(ref, ref, S_RIGHT + 8 * s + 4 * way + 2 * which + u, to)

    def add(r, first=False):
        term = lax.dot_general(
            al[r].reshape(2 * TOK, W),
            at[r].reshape(2 * TOK, W),
            (((0,), (0,)), ((), ())),
            preferred_element_type=F32,
        )
        corr[...] = term if first else corr[...] + term

    def across(n, u):
        ref = piece(at.at[lax.rem(z + (5, 3, 4)[n], 8), xl], u)
        return copy(ref, ref, S_CROSS + 2 * n + u, x_peer)

    def add_pair(s):
        add(lax.rem(z - s + 8, 8))
        add(lax.rem(z + s, 8))

    for u in range(2):

        @pl.when(i != j)
        def _(u=u):
            turn(u).wait_recv()

        for way in range(2):
            start(right_copy(0, way, 0, u))
        start(pair(u))
    for u in range(2):
        pair(u).wait_recv()
        for way in range(2):
            start(right_copy(0, way, 1, u))
    for s, which in ((1, 0), (1, 1), (2, 0)):
        for u in range(2):
            for way in range(2):
                right_copy(s - 1, way, which, u).wait_recv()
                start(right_copy(s, way, which, u))
    run(lambda d: left_pass(1, d), 1, 4)
    run(lambda n: left_forward(n).wait_recv(), 0, 8)
    add(z, True)
    add_pair(1)
    for u in range(2):
        right_copy(2, 0, 0, u).wait_recv()
        start(right_copy(3, 0, 0, u))
        start(across(0, u))
        right_copy(2, 1, 0, u).wait_recv()
        start(across(1, u))
    for u in range(2):
        for way in range(2):
            right_copy(1, way, 1, u).wait_recv()
    add_pair(2)
    for u in range(2):
        right_copy(3, 0, 0, u).wait_recv()
        start(across(2, u))
    for n in range(2):
        for u in range(2):
            across(n, u).wait_recv()
    add_pair(3)
    for u in range(2):
        across(2, u).wait_recv()
    add(lax.rem(z + 4, 8))

    @pl.when(i != j)
    def _():
        turn(0).wait_send()
        turn(1).wait_send()

    drain()


def hand_out(a_l, a_r, corr, a_l_out, a_r_out, corr_out):
    a_l_out[...] = a_l[...]
    a_r_out[...] = a_r[...]
    corr_out[...] = corr[...] * (1.0 / 2048.0)


def per_device(s_l, s_r, g_l, g_r, e_l, e_r, b_l, b_r, p_l, p_r, o_l, o_r):
    vm = pl.BlockSpec(memory_space=pltpu.VMEM)
    hbm = pl.BlockSpec(memory_space=pl.ANY)
    tile = (TOK, W)
    shapes = (
        jax.ShapeDtypeStruct(tile, BF16),
        jax.ShapeDtypeStruct(tile, BF16),
        jax.ShapeDtypeStruct((W, W), F32),
    )
    results = pl.pallas_call(
        kernel,
        out_shape=shapes,
        in_specs=[hbm, hbm, vm, vm, hbm, hbm, vm, vm, hbm, hbm, vm, vm],
        out_specs=(vm, vm, vm),
        scratch_shapes=[
            pltpu.VMEM((8, TOK), F32),
            pltpu.VMEM((8, TOK), F32),
            pltpu.VMEM((16, 8, TOK), F32),
            pltpu.VMEM((8, 8, TOK), F32),
            pltpu.VMEM((2, 2, W, W), BF16),
            pltpu.VMEM((2, HID, W), BF16),
            pltpu.VMEM((W,), F32),
            pltpu.VMEM((W,), F32),
            pltpu.VMEM((2, 8) + tile, BF16),
            pltpu.VMEM((2, 8, 2) + tile, BF16),
            pltpu.VMEM((2, 4, 2, 2) + tile, BF16),
            pltpu.VMEM((2, 4, 2, 2) + tile, BF16),
            pltpu.VMEM((2, 8, 2) + tile, BF16),
            pltpu.VMEM((2, 2, 2, 4) + tile, BF16),
            pltpu.VMEM((2, 2, 4) + tile, BF16),
            pltpu.VMEM((2, 3, 2) + tile, BF16),
            pltpu.VMEM((2, 3, 2) + tile, BF16),
            pltpu.VMEM((2, 2) + tile, BF16),
            pltpu.VMEM((2, 3) + tile, BF16),
            pltpu.VMEM((8, 2) + tile, BF16),
            pltpu.VMEM((8, 2) + tile, BF16),
            pltpu.VMEM((2, 2) + tile, BF16),
            pltpu.VMEM((2, 2048, W), BF16),
            pltpu.VMEM((2, W, HID), BF16),
            pltpu.VMEM((2, HID, W), BF16),
            pltpu.SemaphoreType.DMA((N_SEMS,)),
            pltpu.SemaphoreType.DMA((N_SEMS,)),
            pltpu.SemaphoreType.DMA((10,)),
        ],
        compiler_params=pltpu.CompilerParams(
            collective_id=0, has_side_effects=True, vmem_limit_bytes=56 * 1024 * 1024
        ),
    )(s_l, s_r, g_l, g_r, e_l, e_r, b_l, b_r, p_l, p_r, o_l, o_r)
    return pl.pallas_call(
        hand_out,
        out_shape=shapes,
        in_specs=[vm] * 3,
        out_specs=(vm,) * 3,
    )(*results)


def solution(mesh):
    placed = (
        P(None, "dp"),
        P(None, "dp"),
        P("dp"),
        P("dp"),
        P("dp", "mp"),
        P("dp", "mp"),
        P("mp"),
        P("mp"),
        P("mp", "dp"),
        P("mp", "dp"),
        P("dp"),
        P("dp"),
    )
    return jax.shard_map(
        per_device,
        mesh=mesh,
        in_specs=placed,
        out_specs=(P("mp", "dp"), P("mp", "dp"), P("dp", "mp")),
        check_vma=False,
    )
```
